256 devices in a mesh: blk: 32 (over z, y), lblk: 8 (over x, core).
Axes of the slice: x: 4, y: 4, z: 8, core: 2. Of those that a mesh axis runs over, the one named last changes fastest.
Arguments:
- partial_rows: bfloat16 [8, 32768, 1024], P('lblk', 'blk'), may hold values from -5 to 5
- row_owner: int32 [8, 32768, 1], P('lblk', 'blk'), may hold values from 0 to 31; in each aligned block of 1024 rows (0 to 1023, 1024 to 2047, ..., all dimensions but the last counted through in order) at most 128 rows name the same one
- row_key: int32 [8, 32768], P('lblk', 'blk'), may hold values from 0 to 127
- azimuth_orders: int32 [32], replicated, may hold values from 1 to 4095, as said below
- legendre_table: bfloat16 [32, 4096, 2048], P('blk', 'lblk'), may hold values from -0.125 to 0.125
- spin_even: bfloat16 [32, 4096, 2048], P('blk', 'lblk'), may hold values from -0.125 to 0.125
- spin_odd: bfloat16 [32, 4096, 2048], P('blk', 'lblk'), may hold values from -0.125 to 0.125
Outputs:
- eigenvalues: float32 [2, 2, 8, 256, 8192], P(None, None, 'lblk', 'blk')
- cycle_maps: float32 [2, 8, 256, 8192], P(None, 'lblk', 'blk')
The draws below stay inside these ranges and needn't reach their ends.
Inputs may be any that keep to these rules, and one draw needn't show every extreme that they name: `row_owner`: no more than 128 rows of one device name the same owner; some device sends exactly 128 rows to some owner in every draw. `azimuth_orders`: all distinct; 1 and 4095 are always among them.
All inputs are finite; a program needn't handle non-finite values.
Results may differ from the reference program's by a relative error of at most 0.0041.
Values may be sent and summed in bfloat16 or wider, within the bound.
No kernel may reach another device: no remote copies, remote signals or barrier semaphores. Data moves between devices by JAX's collectives and lax.ppermute only.
A program may use at most 128 MiB of HBM per device.

```python
import math
import jax
import jax.numpy as jnp
import numpy as np
from jax import lax

NPHI = 8192
L = 4096
SEG = 1024
R_DEV = 8
PR = 1024
KEYS = 128
CAP = 128
SLICES = 8
SLICE_CYCLES = 256
CYCLES = 2048
SLICE_ROWS = 32768
M = 32
N_BLK = 32


def draw_azimuth_orders(key, part):
    candidates = jax.random.permutation(jax.random.fold_in(key, 5), L - 3).astype(jnp.int32) + 2
    chosen = jnp.concatenate([candidates[:M - 2], jnp.array([1, L - 1], jnp.int32)])
    return jax.random.permutation(jax.random.fold_in(key, 9), chosen).astype(jnp.int32)


def set_ends(drawn, key, low, top_value):
    longest = drawn.shape.index(max(drawn.shape))
    spots = []
    for shift in (0, 1):
        where = [jax.random.randint(jax.random.fold_in(key, axis), (), 0, length) for axis, length in enumerate(drawn.shape)]
        where[longest] = (where[longest] + shift) % drawn.shape[longest]
        spots.append(tuple(where))
    return drawn.at[spots[0]].set(low).at[spots[1]].set(top_value)


def levels(rng, extent, pieces, smallest, top_value):
    loudness = 1.0
    for axis_at, blocks in pieces:
        heights = jax.random.uniform(jax.random.fold_in(jax.random.fold_in(rng, 6), axis_at), (blocks,), jnp.float32, smallest / len(pieces), top_value / len(pieces))
        loudness = loudness * jnp.repeat(jnp.exp(heights), extent[axis_at] // blocks).reshape((-1,) + (1,) * (len(extent) - 1 - axis_at))
    return loudness


def deal_out(stream_key, own, number, rows, number_of, top, most, lean):
    ranking = jax.random.permutation(stream_key, number_of)
    heavy_load, usual = portions_of(number_of, rows * top, most, lean, True), portions_of(number_of, rows * top, most, lean, False)
    places = jnp.arange(number_of)

    def named(sizes, offset_by):
        used = int((sizes > 0).sum())
        fixed = max(1, used // 4)
        moved = fixed + (places - fixed + offset_by * (used - fixed)) % max(1, number_of - fixed)
        return jnp.zeros((number_of,), jnp.int32).at[ranking[jnp.where(places < fixed, places, moved)]].set(jnp.asarray(sizes, jnp.int32))

    sizes = jnp.where(number % 4 == 0, named(heavy_load, number // 4), named(usual, number - number // 4 - 1))
    mixed = jax.random.permutation(jax.random.fold_in(own, 3), number_of)
    source_of, sink = mixed[0:number_of // 2 * 2:2], mixed[1:number_of // 2 * 2:2]
    margin = jnp.minimum(sizes[source_of] - 1, most - sizes[sink]) // 2
    margin = jnp.where((source_of == ranking[0]) | (sink == ranking[0]) | (sizes[sink] == 0), 0, jnp.maximum(margin, 0))
    moved = jax.random.randint(jax.random.fold_in(own, 4), (number_of // 2,), 0, 1 << 20) % (margin + 1)
    sizes = sizes.at[source_of].add(-moved).at[sink].add(moved)
    items = jnp.searchsorted(jnp.cumsum(sizes), jnp.arange(rows * top), side="right").astype(jnp.int32)
    table = items.reshape(top, rows).T
    table = table[jax.random.permutation(jax.random.fold_in(own, 1), rows)]
    offset_by = jax.random.randint(jax.random.fold_in(own, 2), (rows, 1), 0, top)
    return jnp.take_along_axis(table, (jnp.arange(top)[None, :] + offset_by) % top, axis=1)


def portions_of(amount, total, limit, lean, full):
    loads = [(1 << 20) // math.isqrt(standing ** lean) + 1 for standing in range(1, amount + 1)]
    largest = limit if full else min(limit, max(-(-total // amount), total * loads[0] // sum(loads)))
    least = 1 if total - largest >= amount - 1 else 0
    counts, rest = [largest] + [least] * (amount - 1), total - largest - least * (amount - 1)
    while rest > 0:
        free = [i for i in range(1, amount) if counts[i] < largest] or [i for i in range(1, amount) if counts[i] < limit]
        pool, remaining = sum([loads[i] for i in free]), rest
        for i in free:
            more = min(limit - counts[i], max(1, remaining * loads[i] // pool), rest)
            counts[i] = counts[i] + more
            rest = rest - more
    return np.array(counts)


def gaussian(own_key, dims, spread, most, pieces=(), dtype=jnp.bfloat16):
    entries = jax.random.normal(own_key, dims, jnp.float32) * spread
    if len(pieces) > 0:
        entries = levels(own_key, dims, pieces, -0.22, 0.18) * entries
    return jnp.clip(entries, min=-most, max=most).astype(dtype)


def setup_inputs(seed: int = 0) -> dict:
    seeds = jax.random.split(jax.random.key(seed), 8)
    partial_rows = gaussian(seeds[0], (SLICES, SLICE_ROWS, SEG), 0.35, 5.0, ((0, 8), (1, 32)))
    row_owner_keys = jax.random.split(jax.random.fold_in(seeds[1], 1), SLICES * SLICE_ROWS // PR)
    row_owner_turns = jax.random.permutation(jax.random.fold_in(seeds[1], 3), SLICES * SLICE_ROWS // PR)
    row_owner = jax.vmap(lambda own, number: deal_out(jax.random.fold_in(seeds[1], 2), own, number, PR, N_BLK, 1, CAP, 2))(row_owner_keys, row_owner_turns).reshape((SLICES, SLICE_ROWS, 1))
    row_key = set_ends(jax.random.randint(seeds[2], (SLICES, SLICE_ROWS), 0, KEYS), jax.random.fold_in(seeds[2], 1), 0, KEYS - 1).astype(jnp.int32)
    azimuth_orders = draw_azimuth_orders(jax.random.fold_in(seeds[7], 71), 0)
    legendre_table = gaussian(seeds[4], (M, L, CYCLES), CYCLES ** -0.5, 0.125, ((0, 32), (1, 8)))
    spin_even = gaussian(seeds[5], (M, L, CYCLES), CYCLES ** -0.5, 0.125, ((0, 32), (1, 8)))
    spin_odd = gaussian(seeds[6], (M, L, CYCLES), CYCLES ** -0.5, 0.125, ((0, 32), (1, 8)))
    return {"partial_rows": partial_rows, "row_owner": row_owner, "row_key": row_key, "azimuth_orders": azimuth_orders, "legendre_table": legendre_table, "spin_even": spin_even, "spin_odd": spin_odd}


def wave_table(azimuth_orders, length):
    orders = azimuth_orders.shape[0]
    phase_index = lax.broadcasted_iota(jnp.int32, (orders, length), 1) * azimuth_orders[:, None] % length
    angles = phase_index.astype(jnp.float32) * (2.0 * math.pi / length)
    return jnp.concatenate([jnp.cos(angles), jnp.sin(angles)], axis=0)

def degree_factors(degree):
    smoothing = jnp.exp(-2.0 * degree * (degree + 1.0) / (L * L))
    factor = jnp.sqrt(jnp.maximum((degree - 1.0) * (degree + 2.0), 0.0) / jnp.maximum(degree * (degree + 1.0), 1.0))
    return (smoothing, factor)

def eigen_pair(coefficients, waves):
    orders = coefficients.shape[1]
    real_part = coefficients[..., 0]
    imag_part = coefficients[..., 1]
    real_all = jnp.concatenate([real_part[:, :, :2], -imag_part[:, :, 2:]], axis=2)
    imag_all = jnp.concatenate([imag_part[:, :, :2], real_part[:, :, 2:]], axis=2)
    stacked = jnp.concatenate([real_all, -imag_all], axis=1)
    fields = lax.dot_general(stacked, waves, (((1,), (0,)), ((), ())), precision=lax.Precision.HIGHEST) * (2.0 / math.sqrt(orders))
    half_trace = 0.5 * fields[:, 0]
    shear_size = jnp.sqrt(fields[:, 1] * fields[:, 1] + fields[:, 2] * fields[:, 2])
    return jnp.stack([half_trace + shear_size, half_trace - shear_size], axis=0)

def reference(partial_rows, row_owner, row_key, azimuth_orders, legendre_table, spin_even, spin_odd):
    values = partial_rows.reshape(SLICES * SLICE_ROWS, SEG).astype(jnp.float32)
    slice_index = lax.broadcasted_iota(jnp.int32, (SLICES, SLICE_ROWS), 0)
    target = ((slice_index * N_BLK + row_owner[:, :, 0]) * KEYS + row_key).reshape(-1).astype(jnp.int32)
    blocks = jax.ops.segment_sum(values, target, num_segments=SLICES * N_BLK * KEYS)
    shell_maps = blocks.reshape(SLICES, N_BLK, 2, R_DEV, NPHI).transpose(2, 0, 1, 3, 4)
    cycle_out = shell_maps.reshape(2, SLICES, SLICE_CYCLES, NPHI)
    cycle_maps = shell_maps.reshape(2 * CYCLES, NPHI)
    waves = wave_table(azimuth_orders, NPHI)
    spectra = lax.dot_general(cycle_maps, waves, (((1,), (1,)), ((), ())), precision=lax.Precision.HIGHEST) / math.sqrt(NPHI)
    sign_flip = jnp.array([1.0, -1.0], jnp.float32).reshape(1, 1, 2, 1)
    spectra = spectra.reshape(2, CYCLES, 2, M) * sign_flip
    harmonics = spectra.transpose(3, 0, 2, 1).reshape(M, 4, CYCLES).astype(jnp.bfloat16)
    smoothing, factor = degree_factors(jnp.arange(L).astype(jnp.float32))

    def single_order(operands):
        spectrum, legendre, even_table, odd_table = operands
        coefficients = jnp.dot(legendre, spectrum.T, preferred_element_type=jnp.float32)
        trace_terms = (smoothing[:, None] * coefficients).astype(jnp.bfloat16)
        shear_terms = ((-0.5 * smoothing * factor)[:, None] * coefficients).astype(jnp.bfloat16)
        return jnp.stack([jnp.dot(legendre.T, trace_terms, preferred_element_type=jnp.float32), jnp.dot(even_table.T, shear_terms, preferred_element_type=jnp.float32), jnp.dot(odd_table.T, shear_terms, preferred_element_type=jnp.float32)], axis=1)
    synthesis = lax.map(single_order, (harmonics, legendre_table, spin_even, spin_odd)).astype(jnp.bfloat16)
    coefficients = synthesis.astype(jnp.float32).transpose(1, 0, 2, 3).reshape(CYCLES, M, 3, 2, 2)
    eigen = eigen_pair(coefficients, waves)
    return (eigen.transpose(0, 2, 1, 3).reshape(2, 2, SLICES, SLICE_CYCLES, NPHI), cycle_out)
```

```python
import functools
import math

import jax
import jax.numpy as jnp
from jax import lax
from jax.experimental import pallas as pl
from jax.experimental.pallas import tpu as pltpu
from jax.sharding import Mesh
from jax.sharding import PartitionSpec as P

NPHI = 8192
L = 4096
SEG = 1024
R_DEV = 8
PR = 1024
KEYS = 128
POS = NPHI // SEG
BLK = ("blk_0", "blk_1")
LANES_Y = 1024

NT = (((1,), (1,)), ((), ()))
NN = (((1,), (0,)), ((), ()))


def halves(x):
    high = x.astype(jnp.bfloat16)
    low = (x - high.astype(jnp.float32)).astype(jnp.bfloat16)
    return high, low


def dot32(a, b, dims):
    return lax.dot_general(a, b, dims, preferred_element_type=jnp.float32)


def wave_tables(azimuth_orders):
    phase = lax.broadcasted_iota(jnp.int32, (azimuth_orders.shape[0], SEG), 1)
    phase = phase * azimuth_orders[:, None] % NPHI
    angles = phase.astype(jnp.float32) * (2.0 * math.pi / NPHI)
    return jnp.concatenate([jnp.cos(angles), jnp.sin(angles)], axis=0)


def eighth_turn(index):
    angle = (index & (POS - 1)).astype(jnp.float32) * (2.0 * math.pi / POS)
    return jnp.cos(angle), jnp.sin(angle)


def modes_kernel(slices, rows_ref, owner_ref, key_ref, order_ref, wave_ref, out_ref):
    orders = order_ref.shape[0]
    w_high, w_low = halves(wave_ref[...])
    rows = rows_ref[...]
    seg = dot32(w_high, rows, NT) + dot32(w_low, rows, NT)
    cos_part, sin_part = seg[:orders], seg[orders:]
    key = key_ref[...]
    turn_cos, turn_sin = eighth_turn(order_ref[...] * (key & (POS - 1)))
    modes = jnp.concatenate(
        [
            cos_part * turn_cos - sin_part * turn_sin,
            sin_part * turn_cos + cos_part * turn_sin,
        ],
        axis=0,
    )
    cycles = slices * R_DEV
    slot = (key >> 6) * cycles + owner_ref[...] * R_DEV + ((key >> 3) & (R_DEV - 1))
    pick = lax.broadcasted_iota(jnp.int32, (2 * cycles, PR), 0) == slot
    pick = jnp.where(pick, 1.0, 0.0).astype(jnp.bfloat16)
    m_high, m_low = halves(modes)
    sums = dot32(m_high, pick, NT) + dot32(m_low, pick, NT)
    parts = cycles // 128
    for trig in range(2):
        for shell in range(2):
            for part in range(parts):
                out_ref[:, part * 4 + trig * 2 + shell, :] = sums[
                    trig * orders : (trig + 1) * orders,
                    shell * cycles + part * 128 : shell * cycles + (part + 1) * 128,
                ]


def local_modes(rows, owners, keys, azimuth_orders, waves, groups):
    orders = azimuth_orders.shape[0]
    return pl.pallas_call(
        functools.partial(modes_kernel, groups),
        out_shape=jax.ShapeDtypeStruct((orders, groups * R_DEV * 4 // 128, 128), jnp.float32),
        name="modes",
    )(rows, owners, keys, azimuth_orders[:, None], waves)


def harmonics_kernel(in_ref, out_ref):
    total = jnp.sum(in_ref[...], axis=0) * (1.0 / math.sqrt(NPHI))
    row = lax.broadcasted_iota(jnp.int32, total.shape, 0)
    total = jnp.where((row & 2) == 0, total, -total)
    out_ref[...] = jnp.broadcast_to(total[None], out_ref.shape).astype(out_ref.dtype)


def harmonics_for_all(arrived, copies):
    return pl.pallas_call(
        harmonics_kernel,
        out_shape=jax.ShapeDtypeStruct((copies, *arrived.shape[1:]), jnp.bfloat16),
        name="harmonics",
    )(arrived)


def legendre_kernel(first_ref, modes_ref, leg_ref, even_hbm, odd_hbm, out_ref, even, odd, sem):
    even_copy = pltpu.make_async_copy(even_hbm, even, sem.at[0])
    odd_copy = pltpu.make_async_copy(odd_hbm, odd, sem.at[1])
    even_copy.start()
    odd_copy.start()
    blocks, rows = modes_ref.shape[0], modes_ref.shape[1]
    pieces = []
    for block in range(blocks):
        value = modes_ref[block].astype(jnp.float32)
        for part in range(rows // 4):
            pieces.append(value[part * 4 : (part + 1) * 4])
    spectrum = jnp.concatenate(pieces, axis=1).astype(jnp.bfloat16)
    coefficients = dot32(spectrum, leg_ref[0], NT)
    width = coefficients.shape[1]
    degree = first_ref[0] + lax.broadcasted_iota(jnp.int32, (1, width), 1)
    degree = degree.astype(jnp.float32)
    smoothing = jnp.exp(-2.0 * degree * (degree + 1.0) / (L * L))
    factor = jnp.sqrt(
        jnp.maximum((degree - 1.0) * (degree + 2.0), 0.0)
        / jnp.maximum(degree * (degree + 1.0), 1.0)
    )
    trace_terms = (smoothing * coefficients).astype(jnp.bfloat16)
    shear_terms = ((-0.5 * smoothing * factor) * coefficients).astype(jnp.bfloat16)
    own = out_ref.shape[2]

    def put(kind, value):
        for block in range(blocks):
            out_ref[block, kind * 4 : kind * 4 + 4, :] = value[:, block * own : (block + 1) * own]

    put(0, dot32(trace_terms, leg_ref[0], NN))
    even_copy.wait()
    put(1, dot32(shear_terms, even[0], NN))
    odd_copy.wait()
    put(2, dot32(shear_terms, odd[0], NN))


def legendre_pair(first_degree, modes, legendre_table, spin_even, spin_odd):
    vmem = pl.BlockSpec(memory_space=pltpu.VMEM)
    left = pl.BlockSpec(memory_space=pl.ANY)
    blocks = modes.shape[0]
    cycles = legendre_table.shape[2]
    return pl.pallas_call(
        legendre_kernel,
        out_shape=jax.ShapeDtypeStruct((blocks, 12, cycles // blocks), jnp.float32),
        in_specs=[pl.BlockSpec(memory_space=pltpu.SMEM), vmem, vmem, left, left],
        out_specs=vmem,
        scratch_shapes=[
            pltpu.VMEM(spin_even.shape, spin_even.dtype),
            pltpu.VMEM(spin_odd.shape, spin_odd.dtype),
            pltpu.SemaphoreType.DMA((2,)),
        ],
        name="legendre",
    )(first_degree, modes, legendre_table, spin_even, spin_odd)


def fields_kernel(scale, terms_ref, order_ref, wave_ref, out_ref):
    position = pl.program_id(0)
    turn_cos, turn_sin = eighth_turn(order_ref[...] * position)
    real, imag = [], []
    for kind in range(3):
        for shell in range(2):
            cos_term, sin_term = terms_ref[kind * 4 + shell], terms_ref[kind * 4 + 2 + shell]
            real.append(-sin_term if kind == 2 else cos_term)
            imag.append(cos_term if kind == 2 else sin_term)
    real = jnp.concatenate(real, axis=0)
    imag = jnp.concatenate(imag, axis=0)
    turned = jnp.concatenate(
        [real * turn_cos - imag * turn_sin, -(real * turn_sin + imag * turn_cos)], axis=1
    )
    t_high, t_low = halves(turned)
    w_high, w_low = halves(wave_ref[...])
    fields = (dot32(t_high, w_high, NN) + (dot32(t_high, w_low, NN) + dot32(t_low, w_high, NN))) * scale
    fields = fields.reshape(3, 2, R_DEV, SEG)
    for shell in range(2):
        half_trace = 0.5 * fields[0, shell]
        first, second = fields[1, shell], fields[2, shell]
        size = jnp.sqrt(first * first + second * second)
        out_ref[0, shell, 0] = half_trace + size
        out_ref[1, shell, 0] = half_trace - size


def eigenvalues(terms, azimuth_orders, waves):
    orders = azimuth_orders.shape[0]
    whole = lambda *shape: pl.BlockSpec(shape, lambda p: (0,) * len(shape))
    return pl.pallas_call(
        functools.partial(fields_kernel, 2.0 / math.sqrt(orders)),
        out_shape=jax.ShapeDtypeStruct((2, 2, 1, R_DEV, NPHI), jnp.float32),
        grid=(POS,),
        in_specs=[whole(12, R_DEV, orders), whole(1, orders), whole(2 * orders, SEG)],
        out_specs=pl.BlockSpec((2, 2, 1, R_DEV, SEG), lambda p: (0, 0, 0, 0, p)),
        name="fields",
    )(terms, azimuth_orders[None], waves)


def shifted(x, axis, by):
    size = lax.axis_size(axis)
    return lax.ppermute(x, axis, [(i, (i + by) % size) for i in range(size)])


def ring_sums(chunk, axis):
    size = lax.axis_size(axis)
    middle = size // 2
    half = chunk(middle).shape[0] // 2

    def toward(by, first):
        far = chunk(middle)
        moving = far[:half] if first else far[half:]
        for distance in range(middle - 1, -1, -1):
            moving = shifted(moving.astype(jnp.bfloat16), axis, by).astype(jnp.float32)
            if distance == 0:
                return moving
            own = chunk(distance if by == 1 else size - distance)
            if distance == middle - 1:
                if first:
                    moving = jnp.concatenate([own[:half] + moving, own[half:]], axis=0)
                else:
                    moving = jnp.concatenate([own[:half], own[half:] + moving], axis=0)
            else:
                moving = own + moving

    return chunk(0), toward(1, True), toward(-1, False)


def row_slots(owners, keys):
    place = (keys & 64) + (keys & 7) * R_DEV + ((keys >> 3) & 7)
    return owners * KEYS + place


def picked(slots, base, count, rows):
    pick = lax.broadcasted_iota(jnp.int32, (count, slots.shape[0]), 0) == (slots - base)[None, :]
    return jnp.dot(pick.astype(jnp.bfloat16), rows, preferred_element_type=jnp.float32)


def column_first(rows, owners, keys):
    ny, nz = lax.axis_size(BLK[1]), lax.axis_size(BLK[0])
    my_y, my_z = lax.axis_index(BLK[1]), lax.axis_index(BLK[0])
    slots = row_slots(owners, keys)
    half = PR // 2

    def column_sums(slot, values):
        owner, place = slot // KEYS, slot % KEYS
        distance = (owner // ny - my_z) % nz
        mine = jnp.where(owner % ny == my_y, distance * KEYS + place, -1)
        return picked(mine, 0, nz * KEYS, values)

    up, down = shifted(rows, BLK[1], 1), shifted(rows, BLK[1], -1)
    up_slots, down_slots = shifted(slots, BLK[1], 1), shifted(slots, BLK[1], -1)
    far_slots = shifted(slots, BLK[1], 2)
    up_far = shifted(up[:half], BLK[1], 1)
    down_far = shifted(down[half:], BLK[1], -1)
    sums = column_sums(slots, rows)
    sums = sums + column_sums(up_slots, up)
    sums = sums + column_sums(down_slots, down)
    sums = sums + column_sums(far_slots[:half], up_far)
    sums = sums + column_sums(far_slots[half:], down_far)
    return ring_sums(lambda d: sums[d * KEYS : (d + 1) * KEYS], BLK[0])


def maps_kernel(own_ref, up_ref, down_ref, out_ref):
    total = own_ref[...] + up_ref[...].astype(jnp.float32) + down_ref[...].astype(jnp.float32)
    for shell in range(2):
        for position in range(POS):
            row = (shell * POS + position) * R_DEV
            out_ref[shell, 0, :, position * SEG : (position + 1) * SEG] = total[row : row + R_DEV]


def map_output(own, up, down):
    return pl.pallas_call(
        maps_kernel,
        out_shape=jax.ShapeDtypeStruct((2, 1, R_DEV, NPHI), jnp.float32),
        name="maps",
    )(own, up.astype(jnp.bfloat16), down.astype(jnp.bfloat16))


def body(partial_rows, row_owner, row_key, azimuth_orders, legendre_table, spin_even, spin_odd):
    groups = lax.axis_size(BLK)
    blocks = lax.axis_size("lblk")
    rows = partial_rows[0]
    owners = row_owner[0, :, 0]
    keys = row_key[0]
    orders = azimuth_orders.shape[0]
    waves = wave_tables(azimuth_orders)

    sums = local_modes(rows, owners[None], keys[None], azimuth_orders, waves, groups)
    arrived = lax.all_to_all(sums, BLK, split_axis=0, concat_axis=0, tiled=True)
    modes = lax.all_to_all(harmonics_for_all(arrived, blocks), "lblk", 0, 0, tiled=True)
    first_degree = (lax.axis_index("lblk") * legendre_table.shape[1]).astype(jnp.int32)[None]
    pieces = legendre_pair(first_degree, modes, legendre_table, spin_even, spin_odd)
    pieces = lax.all_to_all(pieces, "lblk", split_axis=0, concat_axis=0, tiled=True)
    summed = pieces.sum(axis=0).astype(jnp.bfloat16)
    summed = summed.reshape(12, groups, R_DEV).transpose(1, 0, 2).reshape(groups, 12 * R_DEV)
    returned = lax.all_to_all(summed, BLK, split_axis=0, concat_axis=0, tiled=True)
    terms = returned.astype(jnp.float32).T.reshape(12, R_DEV, orders)
    eigen = eigenvalues(terms, azimuth_orders, waves)
    return (eigen, map_output(*column_first(rows, owners, keys)))


def solution(mesh):
    finer = Mesh(mesh.devices.reshape(8, 4, mesh.shape["lblk"]), ("blk_0", "blk_1", "lblk"))
    placed = (
        P("lblk", BLK, None),
        P("lblk", BLK, None),
        P("lblk", BLK),
        P(),
        P(BLK, "lblk", None),
        P(BLK, "lblk", None),
        P(BLK, "lblk", None),
    )
    return jax.shard_map(
        body,
        mesh=finer,
        in_specs=placed,
        out_specs=(P(None, None, "lblk", BLK, None), P(None, "lblk", BLK, None)),
        check_vma=False,
    )
```

```python
import functools
import math

import jax
import jax.numpy as jnp
from jax import lax
from jax.experimental import pallas as pl
from jax.experimental.pallas import tpu as pltpu
from jax.sharding import Mesh
from jax.sharding import PartitionSpec as P


NPHI = 8192
L = 4096
SEG = 1024
R_DEV = 8
PR = 1024
KEYS = 128
POS = NPHI // SEG
BLK = ("blk_0", "blk_1")

NT = (((1,), (1,)), ((), ()))
NN = (((1,), (0,)), ((), ()))


def halves(x):
    high = x.astype(jnp.bfloat16)
    low = (x - high.astype(jnp.float32)).astype(jnp.bfloat16)
    return high, low


def dot32(a, b, dims):
    return lax.dot_general(a, b, dims, preferred_element_type=jnp.float32)


def wave_tables(azimuth_orders):
    phase = lax.broadcasted_iota(jnp.int32, (azimuth_orders.shape[0], SEG), 1)
    phase = phase * azimuth_orders[:, None] % NPHI
    angles = phase.astype(jnp.float32) * (2.0 * math.pi / NPHI)
    return jnp.concatenate([jnp.cos(angles), jnp.sin(angles)], axis=0)


def eighth_turn(index):
    angle = (index & (POS - 1)).astype(jnp.float32) * (2.0 * math.pi / POS)
    return jnp.cos(angle), jnp.sin(angle)


def modes_kernel(slices, rows_ref, owner_ref, key_ref, order_ref, wave_ref, out_ref):
    orders = order_ref.shape[0]
    w_high, w_low = halves(wave_ref[...])
    rows = rows_ref[...]
    seg = dot32(w_high, rows, NT) + dot32(w_low, rows, NT)
    cos_part, sin_part = seg[:orders], seg[orders:]
    key = key_ref[...]
    turn_cos, turn_sin = eighth_turn(order_ref[...] * (key & (POS - 1)))
    modes = jnp.concatenate(
        [
            cos_part * turn_cos - sin_part * turn_sin,
            sin_part * turn_cos + cos_part * turn_sin,
        ],
        axis=0,
    )
    cycles = slices * R_DEV
    slot = (key >> 6) * cycles + owner_ref[...] * R_DEV + ((key >> 3) & (R_DEV - 1))
    pick = lax.broadcasted_iota(jnp.int32, (2 * cycles, PR), 0) == slot
    pick = jnp.where(pick, 1.0, 0.0).astype(jnp.bfloat16)
    m_high, m_low = halves(modes)
    sums = dot32(m_high, pick, NT) + dot32(m_low, pick, NT)
    parts = cycles // 128
    for trig in range(2):
        for shell in range(2):
            for part in range(parts):
                out_ref[:, part * 4 + trig * 2 + shell, :] = sums[
                    trig * orders : (trig + 1) * orders,
                    shell * cycles + part * 128 : shell * cycles + (part + 1) * 128,
                ]


def local_modes(rows, owners, keys, azimuth_orders, waves, groups):
    orders = azimuth_orders.shape[0]
    return pl.pallas_call(
        functools.partial(modes_kernel, groups),
        out_shape=jax.ShapeDtypeStruct((orders, groups * R_DEV * 4 // 128, 128), jnp.float32),
        name="modes",
    )(rows, owners, keys, azimuth_orders[:, None], waves)


def harmonics_kernel(in_ref, out_ref):
    total = jnp.sum(in_ref[...], axis=0) * (1.0 / math.sqrt(NPHI))
    row = lax.broadcasted_iota(jnp.int32, total.shape, 0)
    total = jnp.where((row & 2) == 0, total, -total)
    out_ref[...] = jnp.broadcast_to(total[None], out_ref.shape).astype(out_ref.dtype)


def harmonics_for_all(arrived, copies):
    return pl.pallas_call(
        harmonics_kernel,
        out_shape=jax.ShapeDtypeStruct((copies, *arrived.shape[1:]), jnp.bfloat16),
        name="harmonics",
    )(arrived)


def legendre_kernel(first_ref, modes_ref, leg_ref, even_hbm, odd_hbm, out_ref, even, odd, sem):
    even_copy = pltpu.make_async_copy(even_hbm, even, sem.at[0])
    odd_copy = pltpu.make_async_copy(odd_hbm, odd, sem.at[1])
    even_copy.start()
    odd_copy.start()
    blocks, rows = modes_ref.shape[0], modes_ref.shape[1]
    pieces = []
    for block in range(blocks):
        value = modes_ref[block].astype(jnp.float32)
        for part in range(rows // 4):
            pieces.append(value[part * 4 : (part + 1) * 4])
    spectrum = jnp.concatenate(pieces, axis=1).astype(jnp.bfloat16)
    coefficients = dot32(spectrum, leg_ref[0], NT)
    width = coefficients.shape[1]
    degree = first_ref[0] + lax.broadcasted_iota(jnp.int32, (1, width), 1)
    degree = degree.astype(jnp.float32)
    smoothing = jnp.exp(-2.0 * degree * (degree + 1.0) / (L * L))
    factor = jnp.sqrt(
        jnp.maximum((degree - 1.0) * (degree + 2.0), 0.0)
        / jnp.maximum(degree * (degree + 1.0), 1.0)
    )
    trace_terms = (smoothing * coefficients).astype(jnp.bfloat16)
    shear_terms = ((-0.5 * smoothing * factor) * coefficients).astype(jnp.bfloat16)
    own = out_ref.shape[2]

    def put(kind, value):
        for block in range(blocks):
            out_ref[block, kind * 4 : kind * 4 + 4, :] = value[:, block * own : (block + 1) * own]

    put(0, dot32(trace_terms, leg_ref[0], NN))
    even_copy.wait()
    put(1, dot32(shear_terms, even[0], NN))
    odd_copy.wait()
    put(2, dot32(shear_terms, odd[0], NN))


def legendre_pair(first_degree, modes, legendre_table, spin_even, spin_odd):
    vmem = pl.BlockSpec(memory_space=pltpu.VMEM)
    left = pl.BlockSpec(memory_space=pl.ANY)
    blocks = modes.shape[0]
    cycles = legendre_table.shape[2]
    return pl.pallas_call(
        legendre_kernel,
        out_shape=jax.ShapeDtypeStruct((blocks, 12, cycles // blocks), jnp.float32),
        in_specs=[pl.BlockSpec(memory_space=pltpu.SMEM), vmem, vmem, left, left],
        out_specs=vmem,
        scratch_shapes=[
            pltpu.VMEM(spin_even.shape, spin_even.dtype),
            pltpu.VMEM(spin_odd.shape, spin_odd.dtype),
            pltpu.SemaphoreType.DMA((2,)),
        ],
        name="legendre",
    )(first_degree, modes, legendre_table, spin_even, spin_odd)


def fields_kernel(scale, terms_ref, order_ref, wave_ref, out_ref):
    position = pl.program_id(0)
    turn_cos, turn_sin = eighth_turn(order_ref[...] * position)
    real, imag = [], []
    for kind in range(3):
        for shell in range(2):
            cos_term, sin_term = terms_ref[kind * 4 + shell], terms_ref[kind * 4 + 2 + shell]
            real.append(-sin_term if kind == 2 else cos_term)
            imag.append(cos_term if kind == 2 else sin_term)
    real = jnp.concatenate(real, axis=0)
    imag = jnp.concatenate(imag, axis=0)
    turned = jnp.concatenate(
        [real * turn_cos - imag * turn_sin, -(real * turn_sin + imag * turn_cos)], axis=1
    )
    t_high, t_low = halves(turned)
    w_high, w_low = halves(wave_ref[...])
    fields = (dot32(t_high, w_high, NN) + (dot32(t_high, w_low, NN) + dot32(t_low, w_high, NN))) * scale
    fields = fields.reshape(3, 2, R_DEV, SEG)
    for shell in range(2):
        half_trace = 0.5 * fields[0, shell]
        first, second = fields[1, shell], fields[2, shell]
        size = jnp.sqrt(first * first + second * second)
        out_ref[0, shell, 0] = half_trace + size
        out_ref[1, shell, 0] = half_trace - size


def eigenvalues(terms, azimuth_orders, waves):
    orders = azimuth_orders.shape[0]
    whole = lambda *shape: pl.BlockSpec(shape, lambda p: (0,) * len(shape))
    return pl.pallas_call(
        functools.partial(fields_kernel, 2.0 / math.sqrt(orders)),
        out_shape=jax.ShapeDtypeStruct((2, 2, 1, R_DEV, NPHI), jnp.float32),
        grid=(POS,),
        in_specs=[whole(12, R_DEV, orders), whole(1, orders), whole(2 * orders, SEG)],
        out_specs=pl.BlockSpec((2, 2, 1, R_DEV, SEG), lambda p: (0, 0, 0, 0, p)),
        name="fields",
    )(terms, azimuth_orders[None], waves)


def shifted(x, axis, by):
    size = lax.axis_size(axis)
    return lax.ppermute(x, axis, [(i, (i + by) % size) for i in range(size)])


def ring_sums(chunk, axis):
    size = lax.axis_size(axis)
    middle = size // 2
    half = chunk(middle).shape[0] // 2

    def toward(by, first):
        far = chunk(middle)
        moving = far[:half] if first else far[half:]
        for distance in range(middle - 1, -1, -1):
            moving = shifted(moving.astype(jnp.bfloat16), axis, by).astype(jnp.float32)
            if distance == 0:
                return moving
            own = chunk(distance if by == 1 else size - distance)
            if distance == middle - 1:
                if first:
                    moving = jnp.concatenate([own[:half] + moving, own[half:]], axis=0)
                else:
                    moving = jnp.concatenate([own[:half], own[half:] + moving], axis=0)
            else:
                moving = own + moving

    return chunk(0), toward(1, True), toward(-1, False)


def row_slots(owners, keys):
    place = (keys & 64) + (keys & 7) * R_DEV + ((keys >> 3) & 7)
    return owners * KEYS + place


def picked(slots, base, count, rows):
    pick = lax.broadcasted_iota(jnp.int32, (count, slots.shape[0]), 0) == (slots - base)[None, :]
    return jnp.dot(pick.astype(jnp.bfloat16), rows, preferred_element_type=jnp.float32)


def after(x, token):
    return lax.optimization_barrier((x, token))[0]


class ColumnSums:
    def __init__(self, rows, owners, keys):
        self.slots = row_slots(owners, keys)
        self.rows = rows
        half = PR // 2
        axis = BLK[1]
        self.up_slots = shifted(self.slots, axis, 1)
        self.down_slots = shifted(self.slots, axis, -1)
        self.far_slots = shifted(self.slots, axis, 2)
        first, last = rows[:half], rows[half:]
        self.up = [shifted(first, axis, 1), shifted(last, axis, 1)]
        self.down = [shifted(last, axis, -1), shifted(first, axis, -1)]

    def forward(self, token):
        self.up_far = shifted(after(self.up[0], token), BLK[1], 1)
        self.down_far = shifted(after(self.down[0], token), BLK[1], -1)

    def column_sums(self, slot, values):
        ny, nz = lax.axis_size(BLK[1]), lax.axis_size(BLK[0])
        my_y, my_z = lax.axis_index(BLK[1]), lax.axis_index(BLK[0])
        owner, place = slot // KEYS, slot % KEYS
        distance = (owner // ny - my_z) % nz
        mine = jnp.where(owner % ny == my_y, distance * KEYS + place, -1)
        return picked(mine, 0, nz * KEYS, values)

    def finish(self, token):
        half = PR // 2
        up, down, far = self.up_slots, self.down_slots, self.far_slots
        near = self.column_sums(self.slots, self.rows)
        near = near + self.column_sums(up[:half], self.up[0])
        near = near + self.column_sums(down[half:], self.down[0])
        near = near + self.column_sums(up[half:], self.up[1])
        near = near + self.column_sums(down[:half], self.down[1])
        sums = near + self.column_sums(far[:half], self.up_far)
        sums = sums + self.column_sums(far[half:], self.down_far)
        sums = after(sums, token)
        return ring_sums(lambda d: sums[d * KEYS : (d + 1) * KEYS], BLK[0])


def maps_kernel(own_ref, up_ref, down_ref, out_ref):
    total = own_ref[...] + up_ref[...].astype(jnp.float32) + down_ref[...].astype(jnp.float32)
    for shell in range(2):
        for position in range(POS):
            row = (shell * POS + position) * R_DEV
            out_ref[shell, 0, :, position * SEG : (position + 1) * SEG] = total[row : row + R_DEV]


def map_output(own, up, down):
    return pl.pallas_call(
        maps_kernel,
        out_shape=jax.ShapeDtypeStruct((2, 1, R_DEV, NPHI), jnp.float32),
        name="maps",
    )(own, up.astype(jnp.bfloat16), down.astype(jnp.bfloat16))


def body(partial_rows, row_owner, row_key, azimuth_orders, legendre_table, spin_even, spin_odd):
    groups = lax.axis_size(BLK)
    blocks = lax.axis_size("lblk")
    rows = partial_rows[0]
    owners = row_owner[0, :, 0]
    keys = row_key[0]
    orders = azimuth_orders.shape[0]
    waves = wave_tables(azimuth_orders)

    columns = ColumnSums(rows, owners, keys)
    sums = local_modes(rows, owners[None], keys[None], azimuth_orders, waves, groups)
    arrived = lax.all_to_all(sums, BLK, split_axis=0, concat_axis=0, tiled=True)
    columns.forward(arrived)
    modes = harmonics_for_all(arrived, blocks)
    modes = lax.all_to_all(modes, "lblk", 0, 0, tiled=True)
    first_degree = (lax.axis_index("lblk") * legendre_table.shape[1]).astype(jnp.int32)[None]
    pieces = legendre_pair(first_degree, modes, legendre_table, spin_even, spin_odd)
    pieces = lax.all_to_all(pieces, "lblk", split_axis=0, concat_axis=0, tiled=True)
    summed = pieces.sum(axis=0).astype(jnp.bfloat16)
    summed = summed.reshape(12, groups, R_DEV).transpose(1, 0, 2).reshape(groups, 12 * R_DEV)
    returned = lax.all_to_all(summed, BLK, split_axis=0, concat_axis=0, tiled=True)
    terms = returned.astype(jnp.float32).T.reshape(12, R_DEV, orders)
    eigen = eigenvalues(terms, azimuth_orders, waves)
    return (eigen, map_output(*columns.finish(returned)))


def solution(mesh):
    finer = Mesh(mesh.devices.reshape(8, 4, mesh.shape["lblk"]), ("blk_0", "blk_1", "lblk"))
    placed = (
        P("lblk", BLK, None),
        P("lblk", BLK, None),
        P("lblk", BLK),
        P(),
        P(BLK, "lblk", None),
        P(BLK, "lblk", None),
        P(BLK, "lblk", None),
    )
    return jax.shard_map(
        body,
        mesh=finer,
        in_specs=placed,
        out_specs=(P(None, None, "lblk", BLK, None), P(None, "lblk", BLK, None)),
        check_vma=False,
    )
```

```python
import functools
import math

import jax
import jax.numpy as jnp
from jax import lax
from jax.experimental import pallas as pl
from jax.experimental.pallas import tpu as pltpu
from jax.sharding import Mesh
from jax.sharding import PartitionSpec as P


NPHI = 8192
L = 4096
SEG = 1024
R_DEV = 8
PR = 1024
KEYS = 128
POS = NPHI // SEG
BLK = ("blk_0", "blk_1")

NT = (((1,), (1,)), ((), ()))
NN = (((1,), (0,)), ((), ()))


def halves(x):
    high = x.astype(jnp.bfloat16)
    low = (x - high.astype(jnp.float32)).astype(jnp.bfloat16)
    return high, low


def dot32(a, b, dims):
    return lax.dot_general(a, b, dims, preferred_element_type=jnp.float32)


def wave_tables(azimuth_orders):
    phase = lax.broadcasted_iota(jnp.int32, (azimuth_orders.shape[0], SEG), 1)
    phase = phase * azimuth_orders[:, None] % NPHI
    angles = phase.astype(jnp.float32) * (2.0 * math.pi / NPHI)
    return jnp.concatenate([jnp.cos(angles), jnp.sin(angles)], axis=0)


def eighth_turn(index):
    angle = (index & (POS - 1)).astype(jnp.float32) * (2.0 * math.pi / POS)
    return jnp.cos(angle), jnp.sin(angle)


def modes_kernel(slices, rows_ref, owner_ref, key_ref, order_ref, wave_ref, out_ref):
    orders = order_ref.shape[0]
    w_high, w_low = halves(wave_ref[...])
    rows = rows_ref[...]
    seg = dot32(w_high, rows, NT) + dot32(w_low, rows, NT)
    cos_part, sin_part = seg[:orders], seg[orders:]
    key = key_ref[...]
    turn_cos, turn_sin = eighth_turn(order_ref[...] * (key & (POS - 1)))
    modes = jnp.concatenate(
        [
            cos_part * turn_cos - sin_part * turn_sin,
            sin_part * turn_cos + cos_part * turn_sin,
        ],
        axis=0,
    )
    cycles = slices * R_DEV
    slot = (key >> 6) * cycles + owner_ref[...] * R_DEV + ((key >> 3) & (R_DEV - 1))
    pick = lax.broadcasted_iota(jnp.int32, (2 * cycles, PR), 0) == slot
    pick = jnp.where(pick, 1.0, 0.0).astype(jnp.bfloat16)
    m_high, m_low = halves(modes)
    sums = dot32(m_high, pick, NT) + dot32(m_low, pick, NT)
    parts = cycles // 128
    for trig in range(2):
        for shell in range(2):
            for part in range(parts):
                out_ref[:, part * 4 + trig * 2 + shell, :] = sums[
                    trig * orders : (trig + 1) * orders,
                    shell * cycles + part * 128 : shell * cycles + (part + 1) * 128,
                ]


def local_modes(rows, owners, keys, azimuth_orders, waves, groups):
    orders = azimuth_orders.shape[0]
    return pl.pallas_call(
        functools.partial(modes_kernel, groups),
        out_shape=jax.ShapeDtypeStruct((orders, groups * R_DEV * 4 // 128, 128), jnp.float32),
        name="modes",
    )(rows, owners, keys, azimuth_orders[:, None], waves)


def harmonics_kernel(in_ref, out_ref):
    total = jnp.sum(in_ref[...], axis=0) * (1.0 / math.sqrt(NPHI))
    row = lax.broadcasted_iota(jnp.int32, total.shape, 0)
    total = jnp.where((row & 2) == 0, total, -total)
    out_ref[...] = jnp.broadcast_to(total[None], out_ref.shape).astype(out_ref.dtype)


def harmonics_for_all(arrived, copies):
    return pl.pallas_call(
        harmonics_kernel,
        out_shape=jax.ShapeDtypeStruct((copies, *arrived.shape[1:]), jnp.bfloat16),
        name="harmonics",
    )(arrived)


def legendre_kernel(first_ref, modes_ref, leg_ref, even_hbm, odd_hbm, out_ref, even, odd, sem):
    even_copy = pltpu.make_async_copy(even_hbm, even, sem.at[0])
    odd_copy = pltpu.make_async_copy(odd_hbm, odd, sem.at[1])
    even_copy.start()
    odd_copy.start()
    blocks, rows = modes_ref.shape[0], modes_ref.shape[1]
    pieces = []
    for block in range(blocks):
        value = modes_ref[block].astype(jnp.float32)
        for part in range(rows // 4):
            pieces.append(value[part * 4 : (part + 1) * 4])
    spectrum = jnp.concatenate(pieces, axis=1).astype(jnp.bfloat16)
    coefficients = dot32(spectrum, leg_ref[0], NT)
    width = coefficients.shape[1]
    degree = first_ref[0] + lax.broadcasted_iota(jnp.int32, (1, width), 1)
    degree = degree.astype(jnp.float32)
    smoothing = jnp.exp(-2.0 * degree * (degree + 1.0) / (L * L))
    factor = jnp.sqrt(
        jnp.maximum((degree - 1.0) * (degree + 2.0), 0.0)
        / jnp.maximum(degree * (degree + 1.0), 1.0)
    )
    trace_terms = (smoothing * coefficients).astype(jnp.bfloat16)
    shear_terms = ((-0.5 * smoothing * factor) * coefficients).astype(jnp.bfloat16)
    own = out_ref.shape[2]

    def put(kind, value):
        for block in range(blocks):
            out_ref[block, kind * 4 : kind * 4 + 4, :] = value[:, block * own : (block + 1) * own]

    put(0, dot32(trace_terms, leg_ref[0], NN))
    even_copy.wait()
    put(1, dot32(shear_terms, even[0], NN))
    odd_copy.wait()
    put(2, dot32(shear_terms, odd[0], NN))


def legendre_pair(first_degree, modes, legendre_table, spin_even, spin_odd):
    vmem = pl.BlockSpec(memory_space=pltpu.VMEM)
    left = pl.BlockSpec(memory_space=pl.ANY)
    blocks = modes.shape[0]
    cycles = legendre_table.shape[2]
    return pl.pallas_call(
        legendre_kernel,
        out_shape=jax.ShapeDtypeStruct((blocks, 12, cycles // blocks), jnp.float32),
        in_specs=[pl.BlockSpec(memory_space=pltpu.SMEM), vmem, vmem, left, left],
        out_specs=vmem,
        scratch_shapes=[
            pltpu.VMEM(spin_even.shape, spin_even.dtype),
            pltpu.VMEM(spin_odd.shape, spin_odd.dtype),
            pltpu.SemaphoreType.DMA((2,)),
        ],
        name="legendre",
    )(first_degree, modes, legendre_table, spin_even, spin_odd)


def fields_kernel(scale, terms_ref, order_ref, wave_ref, out_ref):
    position = pl.program_id(0)
    turn_cos, turn_sin = eighth_turn(order_ref[...] * position)
    real, imag = [], []
    for kind in range(3):
        for shell in range(2):
            cos_term, sin_term = terms_ref[kind * 4 + shell], terms_ref[kind * 4 + 2 + shell]
            real.append(-sin_term if kind == 2 else cos_term)
            imag.append(cos_term if kind == 2 else sin_term)
    real = jnp.concatenate(real, axis=0)
    imag = jnp.concatenate(imag, axis=0)
    turned = jnp.concatenate(
        [real * turn_cos - imag * turn_sin, -(real * turn_sin + imag * turn_cos)], axis=1
    )
    t_high, t_low = halves(turned)
    w_high, w_low = halves(wave_ref[...])
    fields = (dot32(t_high, w_high, NN) + (dot32(t_high, w_low, NN) + dot32(t_low, w_high, NN))) * scale
    fields = fields.reshape(3, 2, R_DEV, SEG)
    for shell in range(2):
        half_trace = 0.5 * fields[0, shell]
        first, second = fields[1, shell], fields[2, shell]
        size = jnp.sqrt(first * first + second * second)
        out_ref[0, shell, 0] = half_trace + size
        out_ref[1, shell, 0] = half_trace - size


def eigenvalues(terms, azimuth_orders, waves):
    orders = azimuth_orders.shape[0]
    whole = lambda *shape: pl.BlockSpec(shape, lambda p: (0,) * len(shape))
    return pl.pallas_call(
        functools.partial(fields_kernel, 2.0 / math.sqrt(orders)),
        out_shape=jax.ShapeDtypeStruct((2, 2, 1, R_DEV, NPHI), jnp.float32),
        grid=(POS,),
        in_specs=[whole(12, R_DEV, orders), whole(1, orders), whole(2 * orders, SEG)],
        out_specs=pl.BlockSpec((2, 2, 1, R_DEV, SEG), lambda p: (0, 0, 0, 0, p)),
        name="fields",
    )(terms, azimuth_orders[None], waves)


def shifted(x, axis, by):
    size = lax.axis_size(axis)
    return lax.ppermute(x, axis, [(i, (i + by) % size) for i in range(size)])


def ring_sums(chunk, axis, token):
    size = lax.axis_size(axis)
    middle = size // 2
    half = chunk(middle).shape[0] // 2

    def toward(by, first):
        far = chunk(middle)
        moving = far[:half] if first else far[half:]
        for distance in range(middle - 1, -1, -1):
            moving = shifted(moving.astype(jnp.bfloat16), axis, by).astype(jnp.float32)
            if distance == 0:
                return moving
            own = chunk(distance if by == 1 else size - distance)
            if distance == middle - 1:
                own = after(own, token)
                if first:
                    moving = jnp.concatenate([own[:half] + moving, own[half:]], axis=0)
                else:
                    moving = jnp.concatenate([own[:half], own[half:] + moving], axis=0)
            else:
                moving = own + moving

    return chunk(0), toward(1, True), toward(-1, False)


def after(x, token):
    return lax.optimization_barrier((x, token))[0]


DIGIT = 64
EXTRA = 16


def pack_kernel(rows_ref, owner_ref, key_ref, *out_refs):
    size = rows_ref.shape[0] // len(out_refs)
    key = key_ref[...]
    place = (key & 64) + (key & 7) * R_DEV + ((key >> 3) & 7)
    slot = owner_ref[...] * KEYS + place
    for part, out_ref in enumerate(out_refs):
        own = slot[:, part * size : (part + 1) * size]
        row = lax.broadcasted_iota(jnp.int32, (EXTRA, size), 0)
        tail = jnp.where(row == 0, own // DIGIT, jnp.where(row == 1, own % DIGIT, 0))
        out_ref[:size] = rows_ref[part * size : (part + 1) * size]
        out_ref[size:] = jnp.zeros((EXTRA, rows_ref.shape[1]), out_ref.dtype)
        out_ref[size:, :size] = tail.astype(jnp.float32).astype(out_ref.dtype)


def row_pieces(rows, owners, keys, parts):
    piece = jax.ShapeDtypeStruct((rows.shape[0] // parts + EXTRA, rows.shape[1]), rows.dtype)
    return pl.pallas_call(pack_kernel, out_shape=(piece,) * parts, name="pack")(
        rows, owners[None], keys[None]
    )


def sums_kernel(count, has_base, columns, rings, place_ref, *refs):
    pieces, out_ref = refs[:count], refs[-1]
    my_z, my_y = place_ref[0], place_ref[1]
    slots = out_ref.shape[0]
    for index, piece in enumerate(pieces):
        size = piece.shape[0] - EXTRA
        tail = piece[size : size + EXTRA, :size].astype(jnp.float32).astype(jnp.int32)
        slot = tail[0:1] * DIGIT + tail[1:2]
        owner = slot // KEYS
        distance = (owner // columns - my_z) & (rings - 1)
        mine = jnp.where((owner & (columns - 1)) == my_y, distance * KEYS + (slot & (KEYS - 1)), -1)
        pick = lax.broadcasted_iota(jnp.int32, (slots, size), 0) == mine
        pick = jnp.where(pick, 1.0, 0.0).astype(jnp.bfloat16)
        add = dot32(pick, piece[:size], NN)
        if index == 0:
            out_ref[...] = refs[count][...] + add if has_base else add
        else:
            out_ref[...] += add


def sum_pieces(pieces, base, place):
    columns, rings = lax.axis_size(BLK[1]), lax.axis_size(BLK[0])
    smem = pl.BlockSpec(memory_space=pltpu.SMEM)
    vmem = pl.BlockSpec(memory_space=pltpu.VMEM)
    operands = list(pieces) + ([] if base is None else [base])
    return pl.pallas_call(
        functools.partial(sums_kernel, len(pieces), base is not None, columns, rings),
        out_shape=jax.ShapeDtypeStruct((rings * KEYS, pieces[0].shape[1]), jnp.float32),
        in_specs=[smem] + [vmem] * len(operands),
        out_specs=vmem,
    )(place, *operands)


class ColumnSums:
    def __init__(self, rows, owners, keys):
        axis = BLK[1]
        self.place = jnp.stack([lax.axis_index(BLK[0]), lax.axis_index(BLK[1])]).astype(jnp.int32)
        self.pieces = first, last = row_pieces(rows, owners, keys, 2)
        self.up = [shifted(first, axis, 1), shifted(last, axis, 1)]
        self.down = [shifted(last, axis, -1), shifted(first, axis, -1)]

    def forward(self, token):
        self.up_far = shifted(after(self.up[0], token), BLK[1], 1)
        self.down_far = shifted(after(self.down[0], token), BLK[1], -1)

    def finish(self, token):
        sums = sum_pieces(self.pieces, None, self.place)
        sums = sum_pieces(self.up + self.down, sums, self.place)
        sums = sum_pieces([self.up_far, self.down_far], sums, self.place)
        return ring_sums(lambda d: sums[d * KEYS : (d + 1) * KEYS], BLK[0], token)


def maps_kernel(own_ref, up_ref, down_ref, out_ref):
    total = own_ref[...] + up_ref[...].astype(jnp.float32) + down_ref[...].astype(jnp.float32)
    for shell in range(2):
        for position in range(POS):
            row = (shell * POS + position) * R_DEV
            out_ref[shell, 0, :, position * SEG : (position + 1) * SEG] = total[row : row + R_DEV]


def map_output(own, up, down):
    return pl.pallas_call(
        maps_kernel,
        out_shape=jax.ShapeDtypeStruct((2, 1, R_DEV, NPHI), jnp.float32),
        name="maps",
    )(own, up.astype(jnp.bfloat16), down.astype(jnp.bfloat16))


def body(partial_rows, row_owner, row_key, azimuth_orders, legendre_table, spin_even, spin_odd):
    groups = lax.axis_size(BLK)
    blocks = lax.axis_size("lblk")
    rows = partial_rows[0]
    owners = row_owner[0, :, 0]
    keys = row_key[0]
    orders = azimuth_orders.shape[0]
    waves = wave_tables(azimuth_orders)

    columns = ColumnSums(rows, owners, keys)
    sums = local_modes(rows, owners[None], keys[None], azimuth_orders, waves, groups)
    arrived = lax.all_to_all(sums, BLK, split_axis=0, concat_axis=0, tiled=True)
    columns.forward(arrived)
    modes = harmonics_for_all(arrived, blocks)
    modes = lax.all_to_all(modes, "lblk", 0, 0, tiled=True)
    first_degree = (lax.axis_index("lblk") * legendre_table.shape[1]).astype(jnp.int32)[None]
    pieces = legendre_pair(first_degree, modes, legendre_table, spin_even, spin_odd)
    pieces = lax.all_to_all(pieces, "lblk", split_axis=0, concat_axis=0, tiled=True)
    summed = pieces.sum(axis=0).astype(jnp.bfloat16)
    summed = summed.reshape(12, groups, R_DEV).transpose(1, 0, 2).reshape(groups, 12 * R_DEV)
    returned = lax.all_to_all(summed, BLK, split_axis=0, concat_axis=0, tiled=True)
    terms = returned.astype(jnp.float32).T.reshape(12, R_DEV, orders)
    eigen = eigenvalues(terms, azimuth_orders, waves)
    return (eigen, map_output(*columns.finish(returned)))


def solution(mesh):
    finer = Mesh(mesh.devices.reshape(8, 4, mesh.shape["lblk"]), ("blk_0", "blk_1", "lblk"))
    placed = (
        P("lblk", BLK, None),
        P("lblk", BLK, None),
        P("lblk", BLK),
        P(),
        P(BLK, "lblk", None),
        P(BLK, "lblk", None),
        P(BLK, "lblk", None),
    )
    return jax.shard_map(
        body,
        mesh=finer,
        in_specs=placed,
        out_specs=(P(None, None, "lblk", BLK, None), P(None, "lblk", BLK, None)),
        check_vma=False,
    )
```

```python
import functools
import math

import jax
import jax.numpy as jnp
from jax import lax
from jax.experimental import pallas as pl
from jax.experimental.pallas import tpu as pltpu
from jax.sharding import Mesh
from jax.sharding import PartitionSpec as P


NPHI = 8192
L = 4096
SEG = 1024
R_DEV = 8
PR = 1024
KEYS = 128
POS = NPHI // SEG
BLK = ("blk_0", "blk_1")

NT = (((1,), (1,)), ((), ()))
NN = (((1,), (0,)), ((), ()))


def halves(x):
    high = x.astype(jnp.bfloat16)
    low = (x - high.astype(jnp.float32)).astype(jnp.bfloat16)
    return high, low


def dot32(a, b, dims):
    return lax.dot_general(a, b, dims, preferred_element_type=jnp.float32)


def wave_tables(azimuth_orders):
    phase = lax.broadcasted_iota(jnp.int32, (azimuth_orders.shape[0], SEG), 1)
    phase = phase * azimuth_orders[:, None] % NPHI
    angles = phase.astype(jnp.float32) * (2.0 * math.pi / NPHI)
    return jnp.concatenate([jnp.cos(angles), jnp.sin(angles)], axis=0)


def eighth_turn(index):
    angle = (index & (POS - 1)).astype(jnp.float32) * (2.0 * math.pi / POS)
    return jnp.cos(angle), jnp.sin(angle)


def modes_kernel(slices, rows_ref, owner_ref, key_ref, order_ref, wave_ref, out_ref):
    orders = order_ref.shape[0]
    w_high, w_low = halves(wave_ref[...])
    rows = rows_ref[...]
    seg = dot32(w_high, rows, NT) + dot32(w_low, rows, NT)
    cos_part, sin_part = seg[:orders], seg[orders:]
    key = key_ref[...]
    turn_cos, turn_sin = eighth_turn(order_ref[...] * (key & (POS - 1)))
    modes = jnp.concatenate(
        [
            cos_part * turn_cos - sin_part * turn_sin,
            sin_part * turn_cos + cos_part * turn_sin,
        ],
        axis=0,
    )
    cycles = slices * R_DEV
    slot = (key >> 6) * cycles + owner_ref[...] * R_DEV + ((key >> 3) & (R_DEV - 1))
    pick = lax.broadcasted_iota(jnp.int32, (2 * cycles, PR), 0) == slot
    pick = jnp.where(pick, 1.0, 0.0).astype(jnp.bfloat16)
    m_high, m_low = halves(modes)
    sums = dot32(m_high, pick, NT) + dot32(m_low, pick, NT)
    parts = cycles // 128
    for trig in range(2):
        for shell in range(2):
            for part in range(parts):
                out_ref[:, part * 4 + trig * 2 + shell, :] = sums[
                    trig * orders : (trig + 1) * orders,
                    shell * cycles + part * 128 : shell * cycles + (part + 1) * 128,
                ]


def local_modes(rows, owners, keys, azimuth_orders, waves, groups):
    orders = azimuth_orders.shape[0]
    return pl.pallas_call(
        functools.partial(modes_kernel, groups),
        out_shape=jax.ShapeDtypeStruct((orders, groups * R_DEV * 4 // 128, 128), jnp.float32),
        name="modes",
    )(rows, owners, keys, azimuth_orders[:, None], waves)


def harmonics_kernel(in_ref, out_ref):
    total = jnp.sum(in_ref[...], axis=0) * (1.0 / math.sqrt(NPHI))
    row = lax.broadcasted_iota(jnp.int32, total.shape, 0)
    total = jnp.where((row & 2) == 0, total, -total)
    out_ref[...] = jnp.broadcast_to(total[None], out_ref.shape).astype(out_ref.dtype)


def harmonics_for_all(arrived, copies):
    return pl.pallas_call(
        harmonics_kernel,
        out_shape=jax.ShapeDtypeStruct((copies, *arrived.shape[1:]), jnp.bfloat16),
        name="harmonics",
    )(arrived)


def legendre_kernel(first_ref, modes_ref, leg_ref, even_hbm, odd_hbm, out_ref, even, odd, sem):
    even_copy = pltpu.make_async_copy(even_hbm, even, sem.at[0])
    odd_copy = pltpu.make_async_copy(odd_hbm, odd, sem.at[1])
    even_copy.start()
    odd_copy.start()
    blocks, rows = modes_ref.shape[0], modes_ref.shape[1]
    pieces = []
    for block in range(blocks):
        value = modes_ref[block].astype(jnp.float32)
        for part in range(rows // 4):
            pieces.append(value[part * 4 : (part + 1) * 4])
    spectrum = jnp.concatenate(pieces, axis=1).astype(jnp.bfloat16)
    coefficients = dot32(spectrum, leg_ref[0], NT)
    width = coefficients.shape[1]
    degree = first_ref[0] + lax.broadcasted_iota(jnp.int32, (1, width), 1)
    degree = degree.astype(jnp.float32)
    smoothing = jnp.exp(-2.0 * degree * (degree + 1.0) / (L * L))
    factor = jnp.sqrt(
        jnp.maximum((degree - 1.0) * (degree + 2.0), 0.0)
        / jnp.maximum(degree * (degree + 1.0), 1.0)
    )
    trace_terms = (smoothing * coefficients).astype(jnp.bfloat16)
    shear_terms = ((-0.5 * smoothing * factor) * coefficients).astype(jnp.bfloat16)
    own = out_ref.shape[2]

    def put(kind, value):
        for block in range(blocks):
            out_ref[block, kind * 4 : kind * 4 + 4, :] = value[:, block * own : (block + 1) * own]

    put(0, dot32(trace_terms, leg_ref[0], NN))
    even_copy.wait()
    put(1, dot32(shear_terms, even[0], NN))
    odd_copy.wait()
    put(2, dot32(shear_terms, odd[0], NN))


def legendre_pair(first_degree, modes, legendre_table, spin_even, spin_odd):
    vmem = pl.BlockSpec(memory_space=pltpu.VMEM)
    left = pl.BlockSpec(memory_space=pl.ANY)
    blocks = modes.shape[0]
    cycles = legendre_table.shape[2]
    return pl.pallas_call(
        legendre_kernel,
        out_shape=jax.ShapeDtypeStruct((blocks, 12, cycles // blocks), jnp.float32),
        in_specs=[pl.BlockSpec(memory_space=pltpu.SMEM), vmem, vmem, left, left],
        out_specs=vmem,
        scratch_shapes=[
            pltpu.VMEM(spin_even.shape, spin_even.dtype),
            pltpu.VMEM(spin_odd.shape, spin_odd.dtype),
            pltpu.SemaphoreType.DMA((2,)),
        ],
        name="legendre",
    )(first_degree, modes, legendre_table, spin_even, spin_odd)


def fields_kernel(scale, terms_ref, order_ref, wave_ref, out_ref):
    position = pl.program_id(0)
    turn_cos, turn_sin = eighth_turn(order_ref[...] * position)
    real, imag = [], []
    for kind in range(3):
        for shell in range(2):
            cos_term, sin_term = terms_ref[kind * 4 + shell], terms_ref[kind * 4 + 2 + shell]
            real.append(-sin_term if kind == 2 else cos_term)
            imag.append(cos_term if kind == 2 else sin_term)
    real = jnp.concatenate(real, axis=0)
    imag = jnp.concatenate(imag, axis=0)
    turned = jnp.concatenate(
        [real * turn_cos - imag * turn_sin, -(real * turn_sin + imag * turn_cos)], axis=1
    )
    t_high, t_low = halves(turned)
    w_high, w_low = halves(wave_ref[...])
    fields = (dot32(t_high, w_high, NN) + (dot32(t_high, w_low, NN) + dot32(t_low, w_high, NN))) * scale
    fields = fields.reshape(3, 2, R_DEV, SEG)
    for shell in range(2):
        half_trace = 0.5 * fields[0, shell]
        first, second = fields[1, shell], fields[2, shell]
        size = jnp.sqrt(first * first + second * second)
        out_ref[0, shell, 0] = half_trace + size
        out_ref[1, shell, 0] = half_trace - size


def eigenvalues(terms, azimuth_orders, waves):
    orders = azimuth_orders.shape[0]
    whole = lambda *shape: pl.BlockSpec(shape, lambda p: (0,) * len(shape))
    return pl.pallas_call(
        functools.partial(fields_kernel, 2.0 / math.sqrt(orders)),
        out_shape=jax.ShapeDtypeStruct((2, 2, 1, R_DEV, NPHI), jnp.float32),
        grid=(POS,),
        in_specs=[whole(12, R_DEV, orders), whole(1, orders), whole(2 * orders, SEG)],
        out_specs=pl.BlockSpec((2, 2, 1, R_DEV, SEG), lambda p: (0, 0, 0, 0, p)),
        name="fields",
    )(terms, azimuth_orders[None], waves)


def shifted(x, axis, by):
    size = lax.axis_size(axis)
    return lax.ppermute(x, axis, [(i, (i + by) % size) for i in range(size)])


def add_kernel(lead, moving_ref, own_ref, out_ref):
    size = moving_ref.shape[0]
    if size < own_ref.shape[0]:
        other = size if lead == 0 else 0
        out_ref[other : other + size] = own_ref[other : other + size].astype(out_ref.dtype)
    added = own_ref[lead : lead + size] + moving_ref[...].astype(jnp.float32)
    out_ref[lead : lead + size] = added.astype(out_ref.dtype)


def ring_add(moving, own, lead):
    return pl.pallas_call(
        functools.partial(add_kernel, lead),
        out_shape=jax.ShapeDtypeStruct(own.shape, moving.dtype),
        name="ring_add",
    )(moving, own)


def ring_sums(chunks, far, axis, token):
    size = len(chunks)
    middle = size // 2

    def toward(by, moving, lead):
        for distance in range(middle - 1, -1, -1):
            moving = shifted(moving, axis, by)
            if distance == 0:
                return moving
            own = chunks[distance if by == 1 else size - distance]
            if distance == middle - 1:
                moving = ring_add(moving, after(own, token), lead)
            else:
                moving = ring_add(moving, own, 0)

    half = far[0].shape[0]
    return chunks[0], toward(1, far[0], 0), toward(-1, far[1], half)


def after(x, token):
    return lax.optimization_barrier((x, token))[0]


DIGIT = 64
EXTRA = 16


def pack_kernel(rows_hbm, owner_ref, key_ref, *refs):
    tail_ref, sems = refs[-2:]
    outs = refs[:-2]
    size = rows_hbm.shape[0] // len(outs)
    copies = []
    for part, out in enumerate(outs):
        copy = pltpu.make_async_copy(
            rows_hbm.at[pl.ds(part * size, size)], out.at[pl.ds(0, size)], sems.at[part]
        )
        copy.start()
        copies.append(copy)
    key = key_ref[...]
    place = (key & 64) + (key & 7) * R_DEV + ((key >> 3) & 7)
    slot = owner_ref[...] * KEYS + place
    tail_ref[...] = jnp.zeros(tail_ref.shape, tail_ref.dtype)
    for part, out in enumerate(outs):
        own = slot[:, part * size : (part + 1) * size]
        row = lax.broadcasted_iota(jnp.int32, (EXTRA, size), 0)
        tail = jnp.where(row == 0, own // DIGIT, jnp.where(row == 1, own % DIGIT, 0))
        tail_ref[part, :, :size] = tail.astype(jnp.float32).astype(tail_ref.dtype)
        copy = pltpu.make_async_copy(
            tail_ref.at[part], out.at[pl.ds(size, EXTRA)], sems.at[len(outs) + part]
        )
        copy.start()
        copies.append(copy)
    for copy in copies:
        copy.wait()


def row_pieces(rows, owners, keys, parts):
    piece = jax.ShapeDtypeStruct((rows.shape[0] // parts + EXTRA, rows.shape[1]), rows.dtype)
    vmem = pl.BlockSpec(memory_space=pltpu.VMEM)
    left = pl.BlockSpec(memory_space=pl.ANY)
    return pl.pallas_call(
        pack_kernel,
        out_shape=(piece,) * parts,
        in_specs=[left, vmem, vmem],
        out_specs=(left,) * parts,
        scratch_shapes=[
            pltpu.VMEM((parts, EXTRA, rows.shape[1]), rows.dtype),
            pltpu.SemaphoreType.DMA((2 * parts,)),
        ],
        name="pack",
    )(rows, owners[None], keys[None])


def sums_kernel(count, has_base, columns, rings, first, place_ref, *refs):
    pieces, tails = refs[:count], refs[count : 2 * count]
    outs, pick_ref = refs[2 * count + has_base : -1], refs[-1]
    slots = pick_ref.shape[0]
    size = pieces[0].shape[0]

    @pl.when(pl.program_id(0) == 0)
    def _():
        my_z, my_y = place_ref[0], place_ref[1]
        for index, tail_ref in enumerate(tails):
            tail = tail_ref[:, :size].astype(jnp.float32).astype(jnp.int32)
            slot = tail[0:1] * DIGIT + tail[1:2]
            owner = slot // KEYS
            distance = (owner // columns - my_z) & (rings - 1)
            mine = (distance - first) * KEYS + (slot & (KEYS - 1))
            mine = jnp.where((owner & (columns - 1)) == my_y, mine, -1)
            pick = lax.broadcasted_iota(jnp.int32, (slots, size), 0) == mine
            pick_ref[:, index * size : (index + 1) * size] = jnp.where(pick, 1.0, 0.0).astype(
                jnp.bfloat16
            )

    total = refs[2 * count][...] if has_base else 0.0
    for index, piece in enumerate(pieces):
        total = total + dot32(pick_ref[:, index * size : (index + 1) * size], piece[...], NN)
    rows = slots // len(outs)
    for index, out in enumerate(outs):
        out[...] = total[index * rows : (index + 1) * rows].astype(out.dtype)


TILE = 256


def sum_pieces(pieces, base, place, outs, dtype, first=0, chunks=None):
    columns, rings = lax.axis_size(BLK[1]), lax.axis_size(BLK[0])
    chunks = rings if chunks is None else chunks
    size, lanes = pieces[0].shape[0] - EXTRA, pieces[0].shape[1]
    slots = chunks * KEYS
    specs = [pl.BlockSpec(memory_space=pltpu.SMEM)]
    specs += [pl.BlockSpec((size, TILE), lambda n: (0, n)) for _ in pieces]
    specs += [pl.BlockSpec((EXTRA, lanes), lambda n: (size // EXTRA, 0)) for _ in pieces]
    operands = [*pieces, *pieces]
    if base is not None:
        specs.append(pl.BlockSpec((slots, TILE), lambda n: (first // chunks, n)))
        operands.append(base)
    return pl.pallas_call(
        functools.partial(sums_kernel, len(pieces), int(base is not None), columns, rings, first),
        out_shape=tuple(jax.ShapeDtypeStruct((slots // outs, lanes), dtype) for _ in range(outs)),
        grid=(lanes // TILE,),
        in_specs=specs,
        out_specs=tuple(pl.BlockSpec((slots // outs, TILE), lambda n: (0, n)) for _ in range(outs)),
        scratch_shapes=[pltpu.VMEM((slots, size * len(pieces)), jnp.bfloat16)],
    )(place, *operands)


class ColumnSums:
    def __init__(self, rows, owners, keys):
        axis = BLK[1]
        self.place = jnp.stack([lax.axis_index(BLK[0]), lax.axis_index(BLK[1])]).astype(jnp.int32)
        self.pieces = first, last = row_pieces(rows, owners, keys, 2)
        self.up = [shifted(first, axis, 1), shifted(last, axis, 1)]
        self.down = [shifted(last, axis, -1), shifted(first, axis, -1)]

    def forward(self, token):
        self.up_far = shifted(after(self.up[0], token), BLK[1], 1)
        self.down_far = shifted(after(self.down[0], token), BLK[1], -1)

    def finish(self, token):
        def add(pieces, base):
            return sum_pieces(pieces, base, self.place, 1, jnp.float32)[0]

        sums = add(self.pieces, None)
        sums = add([self.up[0], self.down[0]], sums)
        sums = add([self.up[1], self.down[1]], sums)
        rings = lax.axis_size(BLK[0])
        last = [self.up_far, self.down_far]
        far = sum_pieces(last, sums, self.place, 2, jnp.bfloat16, rings // 2, 1)
        chunks = sum_pieces(last, sums, self.place, rings, jnp.float32)
        return ring_sums(chunks, far, BLK[0], token)


def maps_kernel(own_ref, up_ref, down_ref, out_ref):
    total = own_ref[...] + up_ref[...].astype(jnp.float32) + down_ref[...].astype(jnp.float32)
    for shell in range(2):
        for position in range(POS):
            row = (shell * POS + position) * R_DEV
            out_ref[shell, 0, :, position * SEG : (position + 1) * SEG] = total[row : row + R_DEV]


def map_output(own, up, down):
    return pl.pallas_call(
        maps_kernel,
        out_shape=jax.ShapeDtypeStruct((2, 1, R_DEV, NPHI), jnp.float32),
        name="maps",
    )(own, up.astype(jnp.bfloat16), down.astype(jnp.bfloat16))


def body(partial_rows, row_owner, row_key, azimuth_orders, legendre_table, spin_even, spin_odd):
    groups = lax.axis_size(BLK)
    blocks = lax.axis_size("lblk")
    rows = partial_rows[0]
    owners = row_owner[0, :, 0]
    keys = row_key[0]
    orders = azimuth_orders.shape[0]
    waves = wave_tables(azimuth_orders)

    columns = ColumnSums(rows, owners, keys)
    sums = local_modes(rows, owners[None], keys[None], azimuth_orders, waves, groups)
    arrived = lax.all_to_all(sums, BLK, split_axis=0, concat_axis=0, tiled=True)
    columns.forward(arrived)
    modes = harmonics_for_all(arrived, blocks)
    modes = lax.all_to_all(modes, "lblk", 0, 0, tiled=True)
    first_degree = (lax.axis_index("lblk") * legendre_table.shape[1]).astype(jnp.int32)[None]
    pieces = legendre_pair(first_degree, modes, legendre_table, spin_even, spin_odd)
    pieces = lax.all_to_all(pieces, "lblk", split_axis=0, concat_axis=0, tiled=True)
    summed = pieces.sum(axis=0).astype(jnp.bfloat16)
    summed = summed.reshape(12, groups, R_DEV).transpose(1, 0, 2).reshape(groups, 12 * R_DEV)
    returned = lax.all_to_all(summed, BLK, split_axis=0, concat_axis=0, tiled=True)
    terms = returned.astype(jnp.float32).T.reshape(12, R_DEV, orders)
    eigen = eigenvalues(terms, azimuth_orders, waves)
    return (eigen, map_output(*columns.finish(returned)))


def solution(mesh):
    finer = Mesh(mesh.devices.reshape(8, 4, mesh.shape["lblk"]), ("blk_0", "blk_1", "lblk"))
    placed = (
        P("lblk", BLK, None),
        P("lblk", BLK, None),
        P("lblk", BLK),
        P(),
        P(BLK, "lblk", None),
        P(BLK, "lblk", None),
        P(BLK, "lblk", None),
    )
    return jax.shard_map(
        body,
        mesh=finer,
        in_specs=placed,
        out_specs=(P(None, None, "lblk", BLK, None), P(None, "lblk", BLK, None)),
        check_vma=False,
    )
```

```python
import functools
import math

import jax
import jax.numpy as jnp
from jax import lax
from jax.experimental import pallas as pl
from jax.experimental.pallas import tpu as pltpu
from jax.sharding import Mesh
from jax.sharding import PartitionSpec as P


NPHI = 8192
L = 4096
SEG = 1024
R_DEV = 8
PR = 1024
KEYS = 128
POS = NPHI // SEG
BLK = ("blk_0", "blk_1")

NT = (((1,), (1,)), ((), ()))
NN = (((1,), (0,)), ((), ()))


def halves(x):
    high = x.astype(jnp.bfloat16)
    low = (x - high.astype(jnp.float32)).astype(jnp.bfloat16)
    return high, low


def dot32(a, b, dims):
    return lax.dot_general(a, b, dims, preferred_element_type=jnp.float32)


def wave_tables(azimuth_orders):
    phase = lax.broadcasted_iota(jnp.int32, (azimuth_orders.shape[0], SEG), 1)
    phase = phase * azimuth_orders[:, None] % NPHI
    angles = phase.astype(jnp.float32) * (2.0 * math.pi / NPHI)
    return jnp.concatenate([jnp.cos(angles), jnp.sin(angles)], axis=0)


def eighth_turn(index):
    angle = (index & (POS - 1)).astype(jnp.float32) * (2.0 * math.pi / POS)
    return jnp.cos(angle), jnp.sin(angle)


def modes_kernel(slices, rows_ref, owner_ref, key_ref, order_ref, wave_ref, out_ref):
    orders = order_ref.shape[0]
    w_high, w_low = halves(wave_ref[...])
    rows = rows_ref[...]
    seg = dot32(w_high, rows, NT) + dot32(w_low, rows, NT)
    cos_part, sin_part = seg[:orders], seg[orders:]
    key = key_ref[...]
    turn_cos, turn_sin = eighth_turn(order_ref[...] * (key & (POS - 1)))
    modes = jnp.concatenate(
        [
            cos_part * turn_cos - sin_part * turn_sin,
            sin_part * turn_cos + cos_part * turn_sin,
        ],
        axis=0,
    )
    cycles = slices * R_DEV
    slot = (key >> 6) * cycles + owner_ref[...] * R_DEV + ((key >> 3) & (R_DEV - 1))
    pick = lax.broadcasted_iota(jnp.int32, (2 * cycles, PR), 0) == slot
    pick = jnp.where(pick, 1.0, 0.0).astype(jnp.bfloat16)
    m_high, m_low = halves(modes)
    sums = dot32(m_high, pick, NT) + dot32(m_low, pick, NT)
    parts = cycles // 128
    for trig in range(2):
        for shell in range(2):
            for part in range(parts):
                out_ref[:, part * 4 + trig * 2 + shell, :] = sums[
                    trig * orders : (trig + 1) * orders,
                    shell * cycles + part * 128 : shell * cycles + (part + 1) * 128,
                ]


def local_modes(rows, owners, keys, azimuth_orders, waves, groups):
    orders = azimuth_orders.shape[0]
    return pl.pallas_call(
        functools.partial(modes_kernel, groups),
        out_shape=jax.ShapeDtypeStruct((orders, groups * R_DEV * 4 // 128, 128), jnp.float32),
        name="modes",
    )(rows, owners, keys, azimuth_orders[:, None], waves)


def harmonics_kernel(in_ref, out_ref):
    total = jnp.sum(in_ref[...], axis=0) * (1.0 / math.sqrt(NPHI))
    row = lax.broadcasted_iota(jnp.int32, total.shape, 0)
    total = jnp.where((row & 2) == 0, total, -total)
    out_ref[...] = jnp.broadcast_to(total[None], out_ref.shape).astype(out_ref.dtype)


def harmonics_for_all(arrived, copies):
    return pl.pallas_call(
        harmonics_kernel,
        out_shape=jax.ShapeDtypeStruct((copies, *arrived.shape[1:]), jnp.bfloat16),
        name="harmonics",
    )(arrived)


def legendre_kernel(first_ref, modes_ref, leg_ref, even_hbm, odd_hbm, out_ref, even, odd, sem):
    even_copy = pltpu.make_async_copy(even_hbm, even, sem.at[0])
    odd_copy = pltpu.make_async_copy(odd_hbm, odd, sem.at[1])
    even_copy.start()
    odd_copy.start()
    blocks, rows = modes_ref.shape[0], modes_ref.shape[1]
    pieces = []
    for block in range(blocks):
        value = modes_ref[block].astype(jnp.float32)
        for part in range(rows // 4):
            pieces.append(value[part * 4 : (part + 1) * 4])
    spectrum = jnp.concatenate(pieces, axis=1).astype(jnp.bfloat16)
    coefficients = dot32(spectrum, leg_ref[0], NT)
    width = coefficients.shape[1]
    degree = first_ref[0] + lax.broadcasted_iota(jnp.int32, (1, width), 1)
    degree = degree.astype(jnp.float32)
    smoothing = jnp.exp(-2.0 * degree * (degree + 1.0) / (L * L))
    factor = jnp.sqrt(
        jnp.maximum((degree - 1.0) * (degree + 2.0), 0.0)
        / jnp.maximum(degree * (degree + 1.0), 1.0)
    )
    trace_terms = (smoothing * coefficients).astype(jnp.bfloat16)
    shear_terms = ((-0.5 * smoothing * factor) * coefficients).astype(jnp.bfloat16)
    own = out_ref.shape[2]

    def put(kind, value):
        for block in range(blocks):
            out_ref[block, kind * 4 : kind * 4 + 4, :] = value[:, block * own : (block + 1) * own]

    put(0, dot32(trace_terms, leg_ref[0], NN))
    even_copy.wait()
    put(1, dot32(shear_terms, even[0], NN))
    odd_copy.wait()
    put(2, dot32(shear_terms, odd[0], NN))


def legendre_pair(first_degree, modes, legendre_table, spin_even, spin_odd):
    vmem = pl.BlockSpec(memory_space=pltpu.VMEM)
    left = pl.BlockSpec(memory_space=pl.ANY)
    blocks = modes.shape[0]
    cycles = legendre_table.shape[2]
    return pl.pallas_call(
        legendre_kernel,
        out_shape=jax.ShapeDtypeStruct((blocks, 12, cycles // blocks), jnp.float32),
        in_specs=[pl.BlockSpec(memory_space=pltpu.SMEM), vmem, vmem, left, left],
        out_specs=vmem,
        scratch_shapes=[
            pltpu.VMEM(spin_even.shape, spin_even.dtype),
            pltpu.VMEM(spin_odd.shape, spin_odd.dtype),
            pltpu.SemaphoreType.DMA((2,)),
        ],
        name="legendre",
    )(first_degree, modes, legendre_table, spin_even, spin_odd)


def fields_kernel(scale, terms_ref, order_ref, wave_ref, out_ref):
    position = pl.program_id(0)
    turn_cos, turn_sin = eighth_turn(order_ref[...] * position)
    real, imag = [], []
    for kind in range(3):
        for shell in range(2):
            cos_term, sin_term = terms_ref[kind * 4 + shell], terms_ref[kind * 4 + 2 + shell]
            real.append(-sin_term if kind == 2 else cos_term)
            imag.append(cos_term if kind == 2 else sin_term)
    real = jnp.concatenate(real, axis=0)
    imag = jnp.concatenate(imag, axis=0)
    turned = jnp.concatenate(
        [real * turn_cos - imag * turn_sin, -(real * turn_sin + imag * turn_cos)], axis=1
    )
    t_high, t_low = halves(turned)
    w_high, w_low = halves(wave_ref[...])
    fields = (dot32(t_high, w_high, NN) + (dot32(t_high, w_low, NN) + dot32(t_low, w_high, NN))) * scale
    fields = fields.reshape(3, 2, R_DEV, SEG)
    for shell in range(2):
        half_trace = 0.5 * fields[0, shell]
        first, second = fields[1, shell], fields[2, shell]
        size = jnp.sqrt(first * first + second * second)
        out_ref[0, shell, 0] = half_trace + size
        out_ref[1, shell, 0] = half_trace - size


def eigenvalues(terms, azimuth_orders, waves):
    orders = azimuth_orders.shape[0]
    whole = lambda *shape: pl.BlockSpec(shape, lambda p: (0,) * len(shape))
    return pl.pallas_call(
        functools.partial(fields_kernel, 2.0 / math.sqrt(orders)),
        out_shape=jax.ShapeDtypeStruct((2, 2, 1, R_DEV, NPHI), jnp.float32),
        grid=(POS,),
        in_specs=[whole(12, R_DEV, orders), whole(1, orders), whole(2 * orders, SEG)],
        out_specs=pl.BlockSpec((2, 2, 1, R_DEV, SEG), lambda p: (0, 0, 0, 0, p)),
        name="fields",
    )(terms, azimuth_orders[None], waves)


def shifted(x, axis, by):
    size = lax.axis_size(axis)
    return lax.ppermute(x, axis, [(i, (i + by) % size) for i in range(size)])


def add_kernel(up_ref, down_ref, up_own_ref, down_own_ref, up_out, down_out):
    size, whole = up_ref.shape[0], up_own_ref.shape[0]
    for lead, moving_ref, own_ref, out in (
        (0, up_ref, up_own_ref, up_out),
        (whole - size, down_ref, down_own_ref, down_out),
    ):
        if size < whole:
            other = size - lead
            out[other : other + size] = own_ref[other : other + size].astype(out.dtype)
        added = own_ref[lead : lead + size] + moving_ref[...].astype(jnp.float32)
        out[lead : lead + size] = added.astype(out.dtype)


def ring_add(up, down, up_own, down_own):
    lanes = up.shape[1]
    tile = lanes // 2
    own = pl.BlockSpec((up_own.shape[0], tile), lambda n: (0, n))
    moving = pl.BlockSpec((up.shape[0], tile), lambda n: (0, n))
    result = jax.ShapeDtypeStruct(up_own.shape, up.dtype)
    return pl.pallas_call(
        add_kernel,
        out_shape=(result, result),
        grid=(2,),
        in_specs=[moving, moving, own, own],
        out_specs=(own, own),
        name="ring_add",
    )(up, down, up_own, down_own)


def ring_sums(chunks, far, axis, token):
    size = len(chunks)
    middle = size // 2
    up, down = far
    for distance in range(middle - 1, -1, -1):
        up = shifted(up, axis, 1)
        down = shifted(down, axis, -1)
        if distance > 0:
            own = chunks[distance]
            if distance == middle - 1:
                own = after(own, token)
            up, down = ring_add(up, down, own, chunks[size - distance])
    return chunks[0], up, down


def after(x, token):
    return lax.optimization_barrier((x, token))[0]


DIGIT = 64
TILE = 256
EXTRA = 16


def pack_kernel(rows_ref, owner_ref, key_ref, *outs):
    size, lanes = rows_ref.shape[0] // len(outs), rows_ref.shape[1]
    key = key_ref[...]
    place = (key & 64) + (key & 7) * R_DEV + ((key >> 3) & 7)
    slot = owner_ref[...] * KEYS + place
    step = pl.program_id(0)
    row = lax.broadcasted_iota(jnp.int32, (EXTRA, lanes), 0)
    for part, out in enumerate(outs):
        out[:size] = rows_ref[part * size : (part + 1) * size]
        tail = jnp.zeros((EXTRA, lanes), jnp.int32)
        for tile in range(size // lanes):
            start = part * size + tile * lanes
            own = slot[:, start : start + lanes]
            digits = jnp.where(row == 0, own // DIGIT, jnp.where(row == 1, own % DIGIT, 0))
            tail = jnp.where(step == tile, digits, tail)
        out[size:] = tail.astype(jnp.float32).astype(out.dtype)


def row_pieces(rows, owners, keys, parts):
    count, lanes = rows.shape
    piece = jax.ShapeDtypeStruct((count // parts + EXTRA, lanes), rows.dtype)
    line = pl.BlockSpec((1, count), lambda n: (0, 0))
    return pl.pallas_call(
        pack_kernel,
        out_shape=(piece,) * parts,
        grid=(lanes // TILE,),
        in_specs=[pl.BlockSpec((count, TILE), lambda n: (0, n)), line, line],
        out_specs=(pl.BlockSpec((piece.shape[0], TILE), lambda n: (0, n)),) * parts,
        name="pack",
    )(rows, owners[None], keys[None])


def sums_kernel(count, has_base, columns, rings, first, place_ref, *refs):
    pieces, tails = refs[:count], refs[count : 2 * count]
    outs, pick_ref = refs[2 * count + has_base : -1], refs[-1]
    slots = pick_ref.shape[0]
    size = pieces[0].shape[0]

    @pl.when(pl.program_id(0) == 0)
    def _():
        my_z, my_y = place_ref[0], place_ref[1]
        for index, tail_ref in enumerate(tails):
            tail = tail_ref[:, :size].astype(jnp.float32).astype(jnp.int32)
            slot = tail[0:1] * DIGIT + tail[1:2]
            owner = slot // KEYS
            distance = (owner // columns - my_z) & (rings - 1)
            mine = (distance - first) * KEYS + (slot & (KEYS - 1))
            mine = jnp.where((owner & (columns - 1)) == my_y, mine, -1)
            pick = lax.broadcasted_iota(jnp.int32, (slots, size), 0) == mine
            pick_ref[:, index * size : (index + 1) * size] = jnp.where(pick, 1.0, 0.0).astype(
                jnp.bfloat16
            )

    total = refs[2 * count][...] if has_base else 0.0
    for index, piece in enumerate(pieces):
        total = total + dot32(pick_ref[:, index * size : (index + 1) * size], piece[...], NN)
    rows = slots // len(outs)
    for index, out in enumerate(outs):
        out[...] = total[index * rows : (index + 1) * rows].astype(out.dtype)


def sum_pieces(pieces, base, place, outs, dtype, first=0, chunks=None):
    columns, rings = lax.axis_size(BLK[1]), lax.axis_size(BLK[0])
    chunks = rings if chunks is None else chunks
    size, lanes = pieces[0].shape[0] - EXTRA, pieces[0].shape[1]
    slots = chunks * KEYS
    specs = [pl.BlockSpec(memory_space=pltpu.SMEM)]
    specs += [pl.BlockSpec((size, TILE), lambda n: (0, n)) for _ in pieces]
    specs += [pl.BlockSpec((EXTRA, lanes), lambda n: (size // EXTRA, 0)) for _ in pieces]
    operands = [*pieces, *pieces]
    if base is not None:
        specs.append(pl.BlockSpec((slots, TILE), lambda n: (first // chunks, n)))
        operands.append(base)
    return pl.pallas_call(
        functools.partial(sums_kernel, len(pieces), int(base is not None), columns, rings, first),
        out_shape=tuple(jax.ShapeDtypeStruct((slots // outs, lanes), dtype) for _ in range(outs)),
        grid=(lanes // TILE,),
        in_specs=specs,
        out_specs=tuple(pl.BlockSpec((slots // outs, TILE), lambda n: (0, n)) for _ in range(outs)),
        scratch_shapes=[pltpu.VMEM((slots, size * len(pieces)), jnp.bfloat16)],
    )(place, *operands)


class ColumnSums:
    def __init__(self, rows, owners, keys):
        axis = BLK[1]
        self.place = jnp.stack([lax.axis_index(BLK[0]), lax.axis_index(BLK[1])]).astype(jnp.int32)
        self.pieces = first, last = row_pieces(rows, owners, keys, 2)
        self.up = [shifted(first, axis, 1), shifted(last, axis, 1)]
        self.down = [shifted(last, axis, -1), shifted(first, axis, -1)]

    def forward(self, token):
        self.up_far = shifted(after(self.up[0], token), BLK[1], 1)
        self.down_far = shifted(after(self.down[0], token), BLK[1], -1)

    def finish(self, token):
        def add(pieces, base):
            return sum_pieces(pieces, base, self.place, 1, jnp.float32)[0]

        sums = add([*self.pieces, *self.up, *self.down], None)
        rings = lax.axis_size(BLK[0])
        last = [self.up_far, self.down_far]
        far = sum_pieces(last, sums, self.place, 2, jnp.bfloat16, rings // 2, 1)
        chunks = sum_pieces(last, sums, self.place, rings, jnp.float32)
        return ring_sums(chunks, far, BLK[0], token)


def maps_kernel(own_ref, up_ref, down_ref, out_ref):
    total = own_ref[...] + up_ref[...].astype(jnp.float32) + down_ref[...].astype(jnp.float32)
    for shell in range(2):
        for position in range(POS):
            row = (shell * POS + position) * R_DEV
            out_ref[shell, 0, :, position * SEG : (position + 1) * SEG] = total[row : row + R_DEV]


def map_output(own, up, down):
    return pl.pallas_call(
        maps_kernel,
        out_shape=jax.ShapeDtypeStruct((2, 1, R_DEV, NPHI), jnp.float32),
        name="maps",
    )(own, up.astype(jnp.bfloat16), down.astype(jnp.bfloat16))


def body(partial_rows, row_owner, row_key, azimuth_orders, legendre_table, spin_even, spin_odd):
    groups = lax.axis_size(BLK)
    blocks = lax.axis_size("lblk")
    rows = partial_rows[0]
    owners = row_owner[0, :, 0]
    keys = row_key[0]
    orders = azimuth_orders.shape[0]
    waves = wave_tables(azimuth_orders)

    columns = ColumnSums(rows, owners, keys)
    sums = local_modes(rows, owners[None], keys[None], azimuth_orders, waves, groups)
    arrived = lax.all_to_all(sums, BLK, split_axis=0, concat_axis=0, tiled=True)
    columns.forward(arrived)
    modes = harmonics_for_all(arrived, blocks)
    modes = lax.all_to_all(modes, "lblk", 0, 0, tiled=True)
    first_degree = (lax.axis_index("lblk") * legendre_table.shape[1]).astype(jnp.int32)[None]
    pieces = legendre_pair(first_degree, modes, legendre_table, spin_even, spin_odd)
    pieces = lax.all_to_all(pieces, "lblk", split_axis=0, concat_axis=0, tiled=True)
    summed = pieces.sum(axis=0).astype(jnp.bfloat16)
    summed = summed.reshape(12, groups, R_DEV).transpose(1, 0, 2).reshape(groups, 12 * R_DEV)
    returned = lax.all_to_all(summed, BLK, split_axis=0, concat_axis=0, tiled=True)
    terms = returned.astype(jnp.float32).T.reshape(12, R_DEV, orders)
    eigen = eigenvalues(terms, azimuth_orders, waves)
    return (eigen, map_output(*columns.finish(returned)))


def solution(mesh):
    finer = Mesh(mesh.devices.reshape(8, 4, mesh.shape["lblk"]), ("blk_0", "blk_1", "lblk"))
    placed = (
        P("lblk", BLK, None),
        P("lblk", BLK, None),
        P("lblk", BLK),
        P(),
        P(BLK, "lblk", None),
        P(BLK, "lblk", None),
        P(BLK, "lblk", None),
    )
    return jax.shard_map(
        body,
        mesh=finer,
        in_specs=placed,
        out_specs=(P(None, None, "lblk", BLK, None), P(None, "lblk", BLK, None)),
        check_vma=False,
    )
```

```python
import functools
import math

import jax
import jax.numpy as jnp
from jax import lax
from jax.experimental import pallas as pl
from jax.experimental.pallas import tpu as pltpu
from jax.sharding import Mesh
from jax.sharding import PartitionSpec as P


NPHI = 8192
L = 4096
SEG = 1024
R_DEV = 8
PR = 1024
KEYS = 128
POS = NPHI // SEG
BLK = ("blk_0", "blk_1")

NT = (((1,), (1,)), ((), ()))
NN = (((1,), (0,)), ((), ()))


def halves(x):
    high = x.astype(jnp.bfloat16)
    low = (x - high.astype(jnp.float32)).astype(jnp.bfloat16)
    return high, low


def dot32(a, b, dims):
    return lax.dot_general(a, b, dims, preferred_element_type=jnp.float32)


def wave_tables(azimuth_orders):
    orders = azimuth_orders.shape[0]
    trig = lax.broadcasted_iota(jnp.int32, (2, orders, SEG), 0)
    pixel = lax.broadcasted_iota(jnp.int32, (2, orders, SEG), 2)
    phase = pixel * azimuth_orders[None, :, None] - trig * (NPHI // 4)
    angles = (phase & (NPHI - 1)).astype(jnp.float32) * (2.0 * math.pi / NPHI)
    return jnp.cos(angles).reshape(2 * orders, SEG)


def eighth_turn(index):
    angle = (index & (POS - 1)).astype(jnp.float32) * (2.0 * math.pi / POS)
    return jnp.cos(angle), jnp.sin(angle)


def modes_kernel(slices, rows_ref, owner_ref, key_ref, wave_ref, out_ref):
    orders = wave_ref.shape[0] // 2
    w_high, w_low = halves(wave_ref[...])
    rows = rows_ref[...]
    seg = dot32(w_high, rows, NT) + dot32(w_low, rows, NT)
    cos_part, sin_part = seg[:orders], seg[orders:]
    key = key_ref[...]
    half = wave_ref[:, SEG // 2 : SEG // 2 + 1]
    turn_cos, turn_sin = half[:orders], half[orders:]
    for bit in range(3):
        turn_cos, turn_sin = turn_cos * turn_cos - turn_sin * turn_sin, 2.0 * turn_cos * turn_sin
        turned = (key & (1 << bit)) != 0
        step_cos = jnp.where(turned, turn_cos, 1.0)
        step_sin = jnp.where(turned, turn_sin, 0.0)
        cos_part, sin_part = (
            cos_part * step_cos - sin_part * step_sin,
            sin_part * step_cos + cos_part * step_sin,
        )
    modes = jnp.concatenate([cos_part, sin_part], axis=0)
    cycles = slices * R_DEV
    slot = (key >> 6) * cycles + owner_ref[...] * R_DEV + ((key >> 3) & (R_DEV - 1))
    pick = lax.broadcasted_iota(jnp.int32, (2 * cycles, PR), 0) == slot
    pick = jnp.where(pick, 1.0, 0.0).astype(jnp.bfloat16)
    m_high, m_low = halves(modes)
    sums = dot32(m_high, pick, NT) + dot32(m_low, pick, NT)
    parts = cycles // 128
    for trig in range(2):
        for shell in range(2):
            for part in range(parts):
                out_ref[:, part * 4 + trig * 2 + shell, :] = sums[
                    trig * orders : (trig + 1) * orders,
                    shell * cycles + part * 128 : shell * cycles + (part + 1) * 128,
                ]


def local_modes(rows, owners, keys, waves, groups):
    orders = waves.shape[0] // 2
    return pl.pallas_call(
        functools.partial(modes_kernel, groups),
        out_shape=jax.ShapeDtypeStruct((orders, groups * R_DEV * 4 // 128, 128), jnp.float32),
        name="modes",
    )(rows, owners, keys, waves)


def harmonics_kernel(in_ref, out_ref):
    total = jnp.sum(in_ref[...], axis=0) * (1.0 / math.sqrt(NPHI))
    row = lax.broadcasted_iota(jnp.int32, total.shape, 0)
    total = jnp.where((row & 2) == 0, total, -total)
    out_ref[...] = jnp.broadcast_to(total[None], out_ref.shape).astype(out_ref.dtype)


def harmonics_for_all(arrived, copies):
    return pl.pallas_call(
        harmonics_kernel,
        out_shape=jax.ShapeDtypeStruct((copies, *arrived.shape[1:]), jnp.bfloat16),
        name="harmonics",
    )(arrived)


def legendre_kernel(first_ref, modes_ref, leg_ref, even_hbm, odd_hbm, out_ref, even, odd, sem):
    even_copy = pltpu.make_async_copy(even_hbm, even, sem.at[0])
    odd_copy = pltpu.make_async_copy(odd_hbm, odd, sem.at[1])
    even_copy.start()
    odd_copy.start()
    blocks, rows = modes_ref.shape[0], modes_ref.shape[1]
    pieces = []
    for block in range(blocks):
        value = modes_ref[block].astype(jnp.float32)
        for part in range(rows // 4):
            pieces.append(value[part * 4 : (part + 1) * 4])
    spectrum = jnp.concatenate(pieces, axis=1).astype(jnp.bfloat16)
    coefficients = dot32(spectrum, leg_ref[0], NT)
    width = coefficients.shape[1]
    degree = first_ref[0] + lax.broadcasted_iota(jnp.int32, (1, width), 1)
    degree = degree.astype(jnp.float32)
    smoothing = jnp.exp(-2.0 * degree * (degree + 1.0) / (L * L))
    factor = jnp.sqrt(
        jnp.maximum((degree - 1.0) * (degree + 2.0), 0.0)
        / jnp.maximum(degree * (degree + 1.0), 1.0)
    )
    trace_terms = (smoothing * coefficients).astype(jnp.bfloat16)
    shear_terms = ((-0.5 * smoothing * factor) * coefficients).astype(jnp.bfloat16)
    own = out_ref.shape[2]

    def put(kind, value):
        for block in range(blocks):
            out_ref[block, kind * 4 : kind * 4 + 4, :] = value[:, block * own : (block + 1) * own]

    put(0, dot32(trace_terms, leg_ref[0], NN))
    even_copy.wait()
    put(1, dot32(shear_terms, even[0], NN))
    odd_copy.wait()
    put(2, dot32(shear_terms, odd[0], NN))


def legendre_pair(first_degree, modes, legendre_table, spin_even, spin_odd):
    vmem = pl.BlockSpec(memory_space=pltpu.VMEM)
    left = pl.BlockSpec(memory_space=pl.ANY)
    blocks = modes.shape[0]
    cycles = legendre_table.shape[2]
    return pl.pallas_call(
        legendre_kernel,
        out_shape=jax.ShapeDtypeStruct((blocks, 12, cycles // blocks), jnp.float32),
        in_specs=[pl.BlockSpec(memory_space=pltpu.SMEM), vmem, vmem, left, left],
        out_specs=vmem,
        scratch_shapes=[
            pltpu.VMEM(spin_even.shape, spin_even.dtype),
            pltpu.VMEM(spin_odd.shape, spin_odd.dtype),
            pltpu.SemaphoreType.DMA((2,)),
        ],
        name="legendre",
    )(first_degree, modes, legendre_table, spin_even, spin_odd)


def fields_kernel(scale, terms_ref, order_ref, wave_ref, out_ref):
    position = pl.program_id(0)
    turn_cos, turn_sin = eighth_turn(order_ref[...] * position)
    real, imag = [], []
    for kind in range(3):
        for shell in range(2):
            cos_term, sin_term = terms_ref[kind * 4 + shell], terms_ref[kind * 4 + 2 + shell]
            real.append(-sin_term if kind == 2 else cos_term)
            imag.append(cos_term if kind == 2 else sin_term)
    real = jnp.concatenate(real, axis=0)
    imag = jnp.concatenate(imag, axis=0)
    turned = jnp.concatenate(
        [real * turn_cos - imag * turn_sin, -(real * turn_sin + imag * turn_cos)], axis=1
    )
    t_high, t_low = halves(turned)
    w_high, w_low = halves(wave_ref[...])
    fields = (dot32(t_high, w_high, NN) + (dot32(t_high, w_low, NN) + dot32(t_low, w_high, NN))) * scale
    fields = fields.reshape(3, 2, R_DEV, SEG)
    for shell in range(2):
        half_trace = 0.5 * fields[0, shell]
        first, second = fields[1, shell], fields[2, shell]
        size = jnp.sqrt(first * first + second * second)
        out_ref[0, shell, 0] = half_trace + size
        out_ref[1, shell, 0] = half_trace - size


def eigenvalues(terms, azimuth_orders, waves):
    orders = azimuth_orders.shape[0]
    whole = lambda *shape: pl.BlockSpec(shape, lambda p: (0,) * len(shape))
    return pl.pallas_call(
        functools.partial(fields_kernel, 2.0 / math.sqrt(orders)),
        out_shape=jax.ShapeDtypeStruct((2, 2, 1, R_DEV, NPHI), jnp.float32),
        grid=(POS,),
        in_specs=[whole(12, R_DEV, orders), whole(1, orders), whole(2 * orders, SEG)],
        out_specs=pl.BlockSpec((2, 2, 1, R_DEV, SEG), lambda p: (0, 0, 0, 0, p)),
        name="fields",
    )(terms, azimuth_orders[None], waves)


def shifted(x, axis, by):
    size = lax.axis_size(axis)
    return lax.ppermute(x, axis, [(i, (i + by) % size) for i in range(size)])


def add_kernel(up_ref, down_ref, up_own_ref, down_own_ref, up_out, down_out):
    size, whole = up_ref.shape[0], up_own_ref.shape[0]
    for lead, moving_ref, own_ref, out in (
        (0, up_ref, up_own_ref, up_out),
        (whole - size, down_ref, down_own_ref, down_out),
    ):
        if size < whole:
            other = size - lead
            out[other : other + size] = own_ref[other : other + size].astype(out.dtype)
        added = own_ref[lead : lead + size] + moving_ref[...].astype(jnp.float32)
        out[lead : lead + size] = added.astype(out.dtype)


def ring_add(up, down, up_own, down_own):
    lanes = up.shape[1]
    tile = lanes // 2
    own = pl.BlockSpec((up_own.shape[0], tile), lambda n: (0, n))
    moving = pl.BlockSpec((up.shape[0], tile), lambda n: (0, n))
    result = jax.ShapeDtypeStruct(up_own.shape, up.dtype)
    return pl.pallas_call(
        add_kernel,
        out_shape=(result, result),
        grid=(2,),
        in_specs=[moving, moving, own, own],
        out_specs=(own, own),
        name="ring_add",
    )(up, down, up_own, down_own)


def ring_sums(chunks, far, axis, token):
    size = len(chunks)
    middle = size // 2
    up, down = far
    for distance in range(middle - 1, -1, -1):
        up = shifted(up, axis, 1)
        down = shifted(down, axis, -1)
        if distance > 0:
            own = chunks[distance]
            if distance == middle - 1:
                own = after(own, token)
            up, down = ring_add(up, down, own, chunks[size - distance])
    return chunks[0], up, down


def after(x, token):
    return lax.optimization_barrier((x, token))[0]


DIGIT = 64
TILE = 256
EXTRA = 16


def pack_kernel(rows_ref, owner_ref, key_ref, *outs):
    size, lanes = rows_ref.shape[0] // len(outs), rows_ref.shape[1]
    key = key_ref[...]
    place = (key & 64) + (key & 7) * R_DEV + ((key >> 3) & 7)
    slot = owner_ref[...] * KEYS + place
    row = lax.broadcasted_iota(jnp.int32, (EXTRA, size), 0)
    for part, out in enumerate(outs):
        own = slot[:, part * size : (part + 1) * size]
        tail = jnp.where(row == 0, own // DIGIT, jnp.where(row == 1, own % DIGIT, 0))
        out[:size] = rows_ref[part * size : (part + 1) * size]
        out[size:] = jnp.zeros((EXTRA, lanes), out.dtype)
        out[size:, :size] = tail.astype(jnp.float32).astype(out.dtype)


def row_pieces(rows, owners, keys, parts):
    piece = jax.ShapeDtypeStruct((rows.shape[0] // parts + EXTRA, rows.shape[1]), rows.dtype)
    return pl.pallas_call(pack_kernel, out_shape=(piece,) * parts, name="pack")(
        rows, owners[None], keys[None]
    )


def sums_kernel(count, has_base, columns, rings, place_ref, *refs):
    pieces, tails = refs[:count], refs[count : 2 * count]
    outs, pick_ref = refs[2 * count + has_base : -1], refs[-1]
    slots = pick_ref.shape[0]
    size = pieces[0].shape[0]

    @pl.when(pl.program_id(0) == 0)
    def _():
        my_z, my_y = place_ref[0], place_ref[1]
        for index, tail_ref in enumerate(tails):
            tail = tail_ref[:, :size].astype(jnp.float32).astype(jnp.int32)
            slot = tail[0:1] * DIGIT + tail[1:2]
            owner = slot // KEYS
            distance = (owner // columns - my_z) & (rings - 1)
            mine = distance * KEYS + (slot & (KEYS - 1))
            mine = jnp.where((owner & (columns - 1)) == my_y, mine, -1)
            pick = lax.broadcasted_iota(jnp.int32, (slots, size), 0) == mine
            pick_ref[:, index * size : (index + 1) * size] = jnp.where(pick, 1.0, 0.0).astype(
                jnp.bfloat16
            )

    total = refs[2 * count][...] if has_base else 0.0
    for index, piece in enumerate(pieces):
        total = total + dot32(pick_ref[:, index * size : (index + 1) * size], piece[...], NN)
    start = 0
    for out in outs:
        out[...] = total[start : start + out.shape[0]].astype(out.dtype)
        start += out.shape[0]


def sum_pieces(pieces, base, place, outs):
    columns, rings = lax.axis_size(BLK[1]), lax.axis_size(BLK[0])
    size, lanes = pieces[0].shape[0] - EXTRA, pieces[0].shape[1]
    slots = rings * KEYS
    specs = [pl.BlockSpec(memory_space=pltpu.SMEM)]
    specs += [pl.BlockSpec((size, TILE), lambda n: (0, n)) for _ in pieces]
    specs += [pl.BlockSpec((EXTRA, lanes), lambda n: (size // EXTRA, 0)) for _ in pieces]
    operands = [*pieces, *pieces]
    if base is not None:
        specs.append(pl.BlockSpec((slots, TILE), lambda n: (0, n)))
        operands.append(base)
    return pl.pallas_call(
        functools.partial(sums_kernel, len(pieces), int(base is not None), columns, rings),
        out_shape=tuple(jax.ShapeDtypeStruct((rows, lanes), dtype) for rows, dtype in outs),
        grid=(lanes // TILE,),
        in_specs=specs,
        out_specs=tuple(pl.BlockSpec((rows, TILE), lambda n: (0, n)) for rows, _ in outs),
        scratch_shapes=[pltpu.VMEM((slots, size * len(pieces)), jnp.bfloat16)],
    )(place, *operands)


class ColumnSums:
    def __init__(self, rows, owners, keys):
        axis = BLK[1]
        self.place = jnp.stack([lax.axis_index(BLK[0]), lax.axis_index(BLK[1])]).astype(jnp.int32)
        self.pieces = first, last = row_pieces(rows, owners, keys, 2)
        self.up = [shifted(first, axis, 1), shifted(last, axis, 1)]
        self.down = [shifted(last, axis, -1), shifted(first, axis, -1)]

    def forward(self, token):
        self.up_far = shifted(after(self.up[0], token), BLK[1], 1)
        self.down_far = shifted(after(self.down[0], token), BLK[1], -1)

    def finish(self, token):
        rings = lax.axis_size(BLK[0])
        whole = [(rings * KEYS, jnp.float32)]
        (sums,) = sum_pieces(self.pieces, None, self.place, whole)
        (sums,) = sum_pieces([*self.up, *self.down], sums, self.place, whole)
        one, half = (KEYS, jnp.float32), (KEYS // 2, jnp.bfloat16)
        side = [one] * (rings // 2)
        outs = [*side, half, half, *side[1:]]
        parts = sum_pieces([self.up_far, self.down_far], sums, self.place, outs)
        middle = rings // 2
        chunks = [*parts[:middle], None, *parts[middle + 2 :]]
        return ring_sums(chunks, parts[middle : middle + 2], BLK[0], token)


def maps_kernel(own_ref, up_ref, down_ref, out_ref):
    total = own_ref[...] + up_ref[...].astype(jnp.float32) + down_ref[...].astype(jnp.float32)
    for position in range(POS):
        row = position * R_DEV
        out_ref[0, 0, :, position * SEG : (position + 1) * SEG] = total[row : row + R_DEV]


def map_output(own, up, down):
    shell = pl.BlockSpec((KEYS // 2, SEG), lambda s: (s, 0))
    return pl.pallas_call(
        maps_kernel,
        out_shape=jax.ShapeDtypeStruct((2, 1, R_DEV, NPHI), jnp.float32),
        grid=(2,),
        in_specs=[shell, shell, shell],
        out_specs=pl.BlockSpec((1, 1, R_DEV, NPHI), lambda s: (s, 0, 0, 0)),
        name="maps",
    )(own, up, down)


def body(partial_rows, row_owner, row_key, azimuth_orders, legendre_table, spin_even, spin_odd):
    groups = lax.axis_size(BLK)
    blocks = lax.axis_size("lblk")
    rows = partial_rows[0]
    owners = row_owner[0, :, 0]
    keys = row_key[0]
    orders = azimuth_orders.shape[0]
    waves = wave_tables(azimuth_orders)

    columns = ColumnSums(rows, owners, keys)
    sums = local_modes(rows, owners[None], keys[None], waves, groups)
    arrived = lax.all_to_all(sums, BLK, split_axis=0, concat_axis=0, tiled=True)
    columns.forward(arrived)
    modes = harmonics_for_all(arrived, blocks)
    modes = lax.all_to_all(modes, "lblk", 0, 0, tiled=True)
    first_degree = (lax.axis_index("lblk") * legendre_table.shape[1]).astype(jnp.int32)[None]
    pieces = legendre_pair(first_degree, modes, legendre_table, spin_even, spin_odd)
    pieces = lax.all_to_all(pieces, "lblk", split_axis=0, concat_axis=0, tiled=True)
    summed = pieces.sum(axis=0).astype(jnp.bfloat16)
    summed = summed.reshape(12, groups, R_DEV).transpose(1, 0, 2).reshape(groups, 12 * R_DEV)
    returned = lax.all_to_all(summed, BLK, split_axis=0, concat_axis=0, tiled=True)
    terms = returned.astype(jnp.float32).T.reshape(12, R_DEV, orders)
    eigen = eigenvalues(terms, azimuth_orders, waves)
    return (eigen, map_output(*columns.finish(returned)))


def solution(mesh):
    finer = Mesh(mesh.devices.reshape(8, 4, mesh.shape["lblk"]), ("blk_0", "blk_1", "lblk"))
    placed = (
        P("lblk", BLK, None),
        P("lblk", BLK, None),
        P("lblk", BLK),
        P(),
        P(BLK, "lblk", None),
        P(BLK, "lblk", None),
        P(BLK, "lblk", None),
    )
    return jax.shard_map(
        body,
        mesh=finer,
        in_specs=placed,
        out_specs=(P(None, None, "lblk", BLK, None), P(None, "lblk", BLK, None)),
        check_vma=False,
    )
```

```python
import functools
import math

import jax
import jax.numpy as jnp
from jax import lax
from jax.experimental import pallas as pl
from jax.experimental.pallas import tpu as pltpu
from jax.sharding import Mesh
from jax.sharding import PartitionSpec as P


NPHI = 8192
L = 4096
SEG = 1024
R_DEV = 8
PR = 1024
KEYS = 128
POS = NPHI // SEG
BLK = ("blk_0", "blk_1")

NT = (((1,), (1,)), ((), ()))
NN = (((1,), (0,)), ((), ()))


def halves(x):
    high = x.astype(jnp.bfloat16)
    low = (x - high.astype(jnp.float32)).astype(jnp.bfloat16)
    return high, low


def dot32(a, b, dims):
    return lax.dot_general(a, b, dims, preferred_element_type=jnp.float32)


def wave_tables(azimuth_orders):
    orders = azimuth_orders.shape[0]
    trig = lax.broadcasted_iota(jnp.int32, (2, orders, SEG), 0)
    pixel = lax.broadcasted_iota(jnp.int32, (2, orders, SEG), 2)
    phase = pixel * azimuth_orders[None, :, None] - trig * (NPHI // 4)
    angles = (phase & (NPHI - 1)).astype(jnp.float32) * (2.0 * math.pi / NPHI)
    return jnp.cos(angles).reshape(2 * orders, SEG)


def eighth_turn(index):
    angle = (index & (POS - 1)).astype(jnp.float32) * (2.0 * math.pi / POS)
    return jnp.cos(angle), jnp.sin(angle)


def modes_kernel(slices, rows_ref, owner_ref, key_ref, wave_ref, out_ref):
    orders = wave_ref.shape[0] // 2
    w_high, w_low = halves(wave_ref[...])
    rows = rows_ref[...]
    seg = dot32(w_high, rows, NT) + dot32(w_low, rows, NT)
    cos_part, sin_part = seg[:orders], seg[orders:]
    key = key_ref[...]
    half = wave_ref[:, SEG // 2 : SEG // 2 + 1]
    turn_cos, turn_sin = half[:orders], half[orders:]
    for bit in range(3):
        turn_cos, turn_sin = turn_cos * turn_cos - turn_sin * turn_sin, 2.0 * turn_cos * turn_sin
        turned = (key & (1 << bit)) != 0
        step_cos = jnp.where(turned, turn_cos, 1.0)
        step_sin = jnp.where(turned, turn_sin, 0.0)
        cos_part, sin_part = (
            cos_part * step_cos - sin_part * step_sin,
            sin_part * step_cos + cos_part * step_sin,
        )
    modes = jnp.concatenate([cos_part, sin_part], axis=0)
    cycles = slices * R_DEV
    slot = (key >> 6) * cycles + owner_ref[...] * R_DEV + ((key >> 3) & (R_DEV - 1))
    pick = lax.broadcasted_iota(jnp.int32, (2 * cycles, PR), 0) == slot
    pick = jnp.where(pick, 1.0, 0.0).astype(jnp.bfloat16)
    m_high, m_low = halves(modes)
    sums = dot32(m_high, pick, NT) + dot32(m_low, pick, NT)
    parts = cycles // 128
    for trig in range(2):
        for shell in range(2):
            for part in range(parts):
                out_ref[:, part * 4 + trig * 2 + shell, :] = sums[
                    trig * orders : (trig + 1) * orders,
                    shell * cycles + part * 128 : shell * cycles + (part + 1) * 128,
                ]


def local_modes(rows, owners, keys, waves, groups):
    orders = waves.shape[0] // 2
    return pl.pallas_call(
        functools.partial(modes_kernel, groups),
        out_shape=jax.ShapeDtypeStruct((orders, groups * R_DEV * 4 // 128, 128), jnp.float32),
        name="modes",
    )(rows, owners, keys, waves)


def harmonics_kernel(in_ref, out_ref):
    total = jnp.sum(in_ref[...], axis=0) * (1.0 / math.sqrt(NPHI))
    row = lax.broadcasted_iota(jnp.int32, total.shape, 0)
    total = jnp.where((row & 2) == 0, total, -total)
    out_ref[...] = jnp.broadcast_to(total[None], out_ref.shape).astype(out_ref.dtype)


def harmonics_for_all(arrived, copies):
    return pl.pallas_call(
        harmonics_kernel,
        out_shape=jax.ShapeDtypeStruct((copies, *arrived.shape[1:]), jnp.bfloat16),
        in_specs=[pl.BlockSpec(memory_space=pltpu.VMEM)],
        name="harmonics",
    )(in_vmem(arrived))


def legendre_kernel(first_ref, modes_ref, leg_ref, even_hbm, odd_hbm, out_ref, even, odd, sem):
    even_copy = pltpu.make_async_copy(even_hbm, even, sem.at[0])
    odd_copy = pltpu.make_async_copy(odd_hbm, odd, sem.at[1])
    even_copy.start()
    odd_copy.start()
    blocks, rows = modes_ref.shape[0], modes_ref.shape[1]
    pieces = []
    for block in range(blocks):
        value = modes_ref[block].astype(jnp.float32)
        for part in range(rows // 4):
            pieces.append(value[part * 4 : (part + 1) * 4])
    spectrum = jnp.concatenate(pieces, axis=1).astype(jnp.bfloat16)
    coefficients = dot32(spectrum, leg_ref[0], NT)
    width = coefficients.shape[1]
    degree = first_ref[0] + lax.broadcasted_iota(jnp.int32, (1, width), 1)
    degree = degree.astype(jnp.float32)
    smoothing = jnp.exp(-2.0 * degree * (degree + 1.0) / (L * L))
    factor = jnp.sqrt(
        jnp.maximum((degree - 1.0) * (degree + 2.0), 0.0)
        / jnp.maximum(degree * (degree + 1.0), 1.0)
    )
    trace_terms = (smoothing * coefficients).astype(jnp.bfloat16)
    shear_terms = ((-0.5 * smoothing * factor) * coefficients).astype(jnp.bfloat16)
    own = out_ref.shape[2]

    def put(kind, value):
        for block in range(blocks):
            out_ref[block, kind * 4 : kind * 4 + 4, :] = value[:, block * own : (block + 1) * own]

    put(0, dot32(trace_terms, leg_ref[0], NN))
    even_copy.wait()
    put(1, dot32(shear_terms, even[0], NN))
    odd_copy.wait()
    put(2, dot32(shear_terms, odd[0], NN))


def legendre_pair(first_degree, modes, legendre_table, spin_even, spin_odd):
    vmem = pl.BlockSpec(memory_space=pltpu.VMEM)
    left = pl.BlockSpec(memory_space=pl.ANY)
    blocks = modes.shape[0]
    cycles = legendre_table.shape[2]
    return pl.pallas_call(
        legendre_kernel,
        out_shape=jax.ShapeDtypeStruct((blocks, 12, cycles // blocks), jnp.float32),
        in_specs=[pl.BlockSpec(memory_space=pltpu.SMEM), vmem, vmem, left, left],
        out_specs=vmem,
        scratch_shapes=[
            pltpu.VMEM(spin_even.shape, spin_even.dtype),
            pltpu.VMEM(spin_odd.shape, spin_odd.dtype),
            pltpu.SemaphoreType.DMA((2,)),
        ],
        name="legendre",
    )(first_degree, in_vmem(modes), legendre_table, spin_even, spin_odd)


def fields_kernel(scale, terms_ref, order_ref, wave_ref, out_ref):
    position = pl.program_id(0)
    turn_cos, turn_sin = eighth_turn(order_ref[...] * position)
    real, imag = [], []
    for kind in range(3):
        for shell in range(2):
            cos_term, sin_term = terms_ref[kind * 4 + shell], terms_ref[kind * 4 + 2 + shell]
            real.append(-sin_term if kind == 2 else cos_term)
            imag.append(cos_term if kind == 2 else sin_term)
    real = jnp.concatenate(real, axis=0)
    imag = jnp.concatenate(imag, axis=0)
    turned = jnp.concatenate(
        [real * turn_cos - imag * turn_sin, -(real * turn_sin + imag * turn_cos)], axis=1
    )
    t_high, t_low = halves(turned)
    w_high, w_low = halves(wave_ref[...])
    fields = (dot32(t_high, w_high, NN) + (dot32(t_high, w_low, NN) + dot32(t_low, w_high, NN))) * scale
    fields = fields.reshape(3, 2, R_DEV, SEG)
    for shell in range(2):
        half_trace = 0.5 * fields[0, shell]
        first, second = fields[1, shell], fields[2, shell]
        size = jnp.sqrt(first * first + second * second)
        out_ref[0, shell, 0] = half_trace + size
        out_ref[1, shell, 0] = half_trace - size


def eigenvalues(terms, azimuth_orders, waves):
    orders = azimuth_orders.shape[0]
    whole = lambda *shape: pl.BlockSpec(shape, lambda p: (0,) * len(shape))
    return pl.pallas_call(
        functools.partial(fields_kernel, 2.0 / math.sqrt(orders)),
        out_shape=jax.ShapeDtypeStruct((2, 2, 1, R_DEV, NPHI), jnp.float32),
        grid=(POS,),
        in_specs=[whole(12, R_DEV, orders), whole(1, orders), whole(2 * orders, SEG)],
        out_specs=pl.BlockSpec((2, 2, 1, R_DEV, SEG), lambda p: (0, 0, 0, 0, p)),
        name="fields",
    )(terms, azimuth_orders[None], waves)


def shifted(x, axis, by):
    size = lax.axis_size(axis)
    return lax.ppermute(x, axis, [(i, (i + by) % size) for i in range(size)])


def add_kernel(*refs):
    moving, own_hbm, out_hbm = refs[:2], refs[2:4], refs[4:6]
    own, result, sems = refs[6:8], refs[8:10], refs[10]
    size, whole = moving[0].shape[0], own[0].shape[0]
    copies = []
    for side in range(2):
        copies.append(pltpu.make_async_copy(own_hbm[side], own[side], sems.at[side]))
        copies[-1].start()
    sent = []
    for side, lead in ((0, 0), (1, whole - size)):
        copies[side].wait()
        if size < whole:
            other = size - lead
            kept = own[side][other : other + size]
            result[side][other : other + size] = kept.astype(result[side].dtype)
        added = own[side][lead : lead + size] + moving[side][...].astype(jnp.float32)
        result[side][lead : lead + size] = added.astype(result[side].dtype)
        sent.append(pltpu.make_async_copy(result[side], out_hbm[side], sems.at[2 + side]))
        sent[-1].start()
    for copy in sent:
        copy.wait()


def in_vmem(x):
    return pltpu.with_memory_space_constraint(x, pltpu.VMEM)


def ring_add(up, down, up_own, down_own):
    vmem = pl.BlockSpec(memory_space=pltpu.VMEM)
    hbm = pl.BlockSpec(memory_space=pltpu.HBM)
    result = jax.ShapeDtypeStruct(up_own.shape, up.dtype)
    return pl.pallas_call(
        add_kernel,
        out_shape=(result, result),
        in_specs=[vmem, vmem, hbm, hbm],
        out_specs=(hbm, hbm),
        scratch_shapes=[pltpu.VMEM(up_own.shape, up_own.dtype)] * 2
        + [pltpu.VMEM(up_own.shape, up.dtype)] * 2
        + [pltpu.SemaphoreType.DMA((4,))],
        name="ring_add",
    )(in_vmem(up), in_vmem(down), up_own, down_own)


def ring_sums(chunks, far, axis, token):
    size = len(chunks)
    middle = size // 2
    up, down = far
    for distance in range(middle - 1, -1, -1):
        up = shifted(up, axis, 1)
        down = shifted(down, axis, -1)
        if distance > 0:
            own = chunks[distance]
            if distance == middle - 1:
                own = after(own, token)
            up, down = ring_add(up, down, own, chunks[size - distance])
    return chunks[0], up, down


def after(x, token):
    return lax.optimization_barrier((x, token))[0]


DIGIT = 64
TILE = 256
EXTRA = 16


def pack_kernel(rows_ref, owner_ref, key_ref, *outs):
    size, lanes = rows_ref.shape[0] // len(outs), rows_ref.shape[1]
    key = key_ref[...]
    place = (key & 64) + (key & 7) * R_DEV + ((key >> 3) & 7)
    slot = owner_ref[...] * KEYS + place
    row = lax.broadcasted_iota(jnp.int32, (EXTRA, size), 0)
    for part, out in enumerate(outs):
        own = slot[:, part * size : (part + 1) * size]
        tail = jnp.where(row == 0, own // DIGIT, jnp.where(row == 1, own % DIGIT, 0))
        out[:size] = rows_ref[part * size : (part + 1) * size]
        out[size:] = jnp.zeros((EXTRA, lanes), out.dtype)
        out[size:, :size] = tail.astype(jnp.float32).astype(out.dtype)


def row_pieces(rows, owners, keys, parts):
    piece = jax.ShapeDtypeStruct((rows.shape[0] // parts + EXTRA, rows.shape[1]), rows.dtype)
    return pl.pallas_call(pack_kernel, out_shape=(piece,) * parts, name="pack")(
        rows, owners[None], keys[None]
    )


def sums_kernel(count, has_base, columns, rings, place_ref, *refs):
    pieces, tails = refs[:count], refs[count : 2 * count]
    outs, pick_ref = refs[2 * count + has_base : -1], refs[-1]
    slots = pick_ref.shape[0]
    size = pieces[0].shape[0]

    @pl.when(pl.program_id(0) == 0)
    def _():
        my_z, my_y = place_ref[0], place_ref[1]
        for index, tail_ref in enumerate(tails):
            tail = tail_ref[:, :size].astype(jnp.float32).astype(jnp.int32)
            slot = tail[0:1] * DIGIT + tail[1:2]
            owner = slot // KEYS
            distance = (owner // columns - my_z) & (rings - 1)
            mine = distance * KEYS + (slot & (KEYS - 1))
            mine = jnp.where((owner & (columns - 1)) == my_y, mine, -1)
            pick = lax.broadcasted_iota(jnp.int32, (slots, size), 0) == mine
            pick_ref[:, index * size : (index + 1) * size] = jnp.where(pick, 1.0, 0.0).astype(
                jnp.bfloat16
            )

    total = refs[2 * count][...] if has_base else 0.0
    for index, piece in enumerate(pieces):
        total = total + dot32(pick_ref[:, index * size : (index + 1) * size], piece[...], NN)
    start = 0
    for out in outs:
        out[...] = total[start : start + out.shape[0]].astype(out.dtype)
        start += out.shape[0]


def sum_pieces(pieces, base, place, outs):
    columns, rings = lax.axis_size(BLK[1]), lax.axis_size(BLK[0])
    size, lanes = pieces[0].shape[0] - EXTRA, pieces[0].shape[1]
    slots = rings * KEYS
    specs = [pl.BlockSpec(memory_space=pltpu.SMEM)]
    specs += [pl.BlockSpec((size, TILE), lambda n: (0, n)) for _ in pieces]
    specs += [pl.BlockSpec((EXTRA, lanes), lambda n: (size // EXTRA, 0)) for _ in pieces]
    operands = [*pieces, *pieces]
    if base is not None:
        specs.append(pl.BlockSpec((slots, TILE), lambda n: (0, n)))
        operands.append(base)
    return pl.pallas_call(
        functools.partial(sums_kernel, len(pieces), int(base is not None), columns, rings),
        out_shape=tuple(jax.ShapeDtypeStruct((rows, lanes), dtype) for rows, dtype in outs),
        grid=(lanes // TILE,),
        in_specs=specs,
        out_specs=tuple(pl.BlockSpec((rows, TILE), lambda n: (0, n)) for rows, _ in outs),
        scratch_shapes=[pltpu.VMEM((slots, size * len(pieces)), jnp.bfloat16)],
    )(place, *operands)


class ColumnSums:
    def __init__(self, rows, owners, keys, waves):
        axis = BLK[1]
        self.place = jnp.stack([lax.axis_index(BLK[0]), lax.axis_index(BLK[1])]).astype(jnp.int32)
        self.pieces = first, last = row_pieces(rows, owners, keys, 2)
        self.up = [shifted(first, axis, 1), shifted(last, axis, 1)]
        self.down = [shifted(after(last, waves), axis, -1), shifted(first, axis, -1)]

    def forward(self, token):
        self.up_far = shifted(after(self.up[0], token), BLK[1], 1)
        self.down_far = shifted(after(self.down[0], token), BLK[1], -1)

    def finish(self, token):
        rings = lax.axis_size(BLK[0])
        whole = [(rings * KEYS, jnp.float32)]
        (sums,) = sum_pieces(self.pieces, None, self.place, whole)
        near, following = [self.up[0], self.down[0]], [self.up[1], self.down[1]]
        (sums,) = sum_pieces(near, sums, self.place, whole)
        (sums,) = sum_pieces(following, sums, self.place, whole)
        one, half = (KEYS, jnp.float32), (KEYS // 2, jnp.bfloat16)
        side = [one] * (rings // 2)
        outs = [*side, half, half, *side[1:]]
        parts = sum_pieces([self.up_far, self.down_far], sums, self.place, outs)
        middle = rings // 2
        chunks = [*parts[:middle], None, *parts[middle + 2 :]]
        return ring_sums(chunks, parts[middle : middle + 2], BLK[0], token)


def maps_kernel(own, up, down, out_ref):
    for shell in range(2):
        for position in range(POS):
            row = pl.ds((shell * POS + position) * R_DEV, R_DEV)
            total = own[row] + up[row].astype(jnp.float32) + down[row].astype(jnp.float32)
            out_ref[shell, 0, :, position * SEG : (position + 1) * SEG] = total


def map_output(own, up, down):
    vmem = pl.BlockSpec(memory_space=pltpu.VMEM)
    return pl.pallas_call(
        maps_kernel,
        out_shape=jax.ShapeDtypeStruct((2, 1, R_DEV, NPHI), jnp.float32),
        in_specs=[vmem] * 3,
        name="maps",
    )(own, in_vmem(up), in_vmem(down))


def body(partial_rows, row_owner, row_key, azimuth_orders, legendre_table, spin_even, spin_odd):
    groups = lax.axis_size(BLK)
    blocks = lax.axis_size("lblk")
    rows = partial_rows[0]
    owners = row_owner[0, :, 0]
    keys = row_key[0]
    orders = azimuth_orders.shape[0]
    waves = wave_tables(azimuth_orders)

    columns = ColumnSums(rows, owners, keys, waves)
    sums = local_modes(rows, owners[None], keys[None], waves, groups)
    arrived = lax.all_to_all(sums, BLK, split_axis=0, concat_axis=0, tiled=True)
    columns.forward(arrived)
    modes = harmonics_for_all(arrived, blocks)
    modes = lax.all_to_all(modes, "lblk", 0, 0, tiled=True)
    first_degree = (lax.axis_index("lblk") * legendre_table.shape[1]).astype(jnp.int32)[None]
    pieces = legendre_pair(first_degree, modes, legendre_table, spin_even, spin_odd)
    pieces = lax.all_to_all(pieces, "lblk", split_axis=0, concat_axis=0, tiled=True)
    summed = pieces.sum(axis=0).astype(jnp.bfloat16)
    summed = summed.reshape(12, groups, R_DEV).transpose(1, 0, 2).reshape(groups, 12 * R_DEV)
    returned = lax.all_to_all(summed, BLK, split_axis=0, concat_axis=0, tiled=True)
    terms = returned.astype(jnp.float32).T.reshape(12, R_DEV, orders)
    eigen = eigenvalues(terms, azimuth_orders, waves)
    return (eigen, map_output(*columns.finish(returned)))


def solution(mesh):
    finer = Mesh(mesh.devices.reshape(8, 4, mesh.shape["lblk"]), ("blk_0", "blk_1", "lblk"))
    placed = (
        P("lblk", BLK, None),
        P("lblk", BLK, None),
        P("lblk", BLK),
        P(),
        P(BLK, "lblk", None),
        P(BLK, "lblk", None),
        P(BLK, "lblk", None),
    )
    return jax.shard_map(
        body,
        mesh=finer,
        in_specs=placed,
        out_specs=(P(None, None, "lblk", BLK, None), P(None, "lblk", BLK, None)),
        check_vma=False,
    )
```

```python
import functools
import math

import jax
import jax.numpy as jnp
from jax import lax
from jax.experimental import pallas as pl
from jax.experimental.pallas import tpu as pltpu
from jax.sharding import Mesh
from jax.sharding import PartitionSpec as P


NPHI = 8192
L = 4096
SEG = 1024
R_DEV = 8
PR = 1024
KEYS = 128
POS = NPHI // SEG
BLK = ("blk_0", "blk_1")

NT = (((1,), (1,)), ((), ()))
NN = (((1,), (0,)), ((), ()))


def room(mebibytes):
    return pltpu.CompilerParams(vmem_limit_bytes=mebibytes << 20)


def halves(x):
    high = x.astype(jnp.bfloat16)
    low = (x - high.astype(jnp.float32)).astype(jnp.bfloat16)
    return high, low


def dot32(a, b, dims):
    return lax.dot_general(a, b, dims, preferred_element_type=jnp.float32)


def wave_tables(azimuth_orders):
    orders = azimuth_orders.shape[0]
    trig = lax.broadcasted_iota(jnp.int32, (2, orders, SEG), 0)
    pixel = lax.broadcasted_iota(jnp.int32, (2, orders, SEG), 2)
    phase = pixel * azimuth_orders[None, :, None] - trig * (NPHI // 4)
    angles = (phase & (NPHI - 1)).astype(jnp.float32) * (2.0 * math.pi / NPHI)
    return jnp.cos(angles).reshape(2 * orders, SEG)


def eighth_turn(index):
    angle = (index & (POS - 1)).astype(jnp.float32) * (2.0 * math.pi / POS)
    return jnp.cos(angle), jnp.sin(angle)


def modes_kernel(slices, rows_ref, owner_ref, key_ref, wave_ref, out_ref):
    orders = wave_ref.shape[0] // 2
    w_high, w_low = halves(wave_ref[...])
    rows = rows_ref[...]
    seg = dot32(w_high, rows, NT) + dot32(w_low, rows, NT)
    cos_part, sin_part = seg[:orders], seg[orders:]
    key = key_ref[...]
    half = wave_ref[:, SEG // 2 : SEG // 2 + 1]
    turn_cos, turn_sin = half[:orders], half[orders:]
    for bit in range(3):
        turn_cos, turn_sin = turn_cos * turn_cos - turn_sin * turn_sin, 2.0 * turn_cos * turn_sin
        turned = (key & (1 << bit)) != 0
        step_cos = jnp.where(turned, turn_cos, 1.0)
        step_sin = jnp.where(turned, turn_sin, 0.0)
        cos_part, sin_part = (
            cos_part * step_cos - sin_part * step_sin,
            sin_part * step_cos + cos_part * step_sin,
        )
    modes = jnp.concatenate([cos_part, sin_part], axis=0)
    cycles = slices * R_DEV
    slot = (key >> 6) * cycles + owner_ref[...] * R_DEV + ((key >> 3) & (R_DEV - 1))
    pick = lax.broadcasted_iota(jnp.int32, (2 * cycles, PR), 0) == slot
    pick = jnp.where(pick, 1.0, 0.0).astype(jnp.bfloat16)
    m_high, m_low = halves(modes)
    sums = dot32(m_high, pick, NT) + dot32(m_low, pick, NT)
    parts = cycles // 128
    for trig in range(2):
        for shell in range(2):
            for part in range(parts):
                out_ref[:, part * 4 + trig * 2 + shell, :] = sums[
                    trig * orders : (trig + 1) * orders,
                    shell * cycles + part * 128 : shell * cycles + (part + 1) * 128,
                ]


def local_modes(rows, owners, keys, waves, groups):
    orders = waves.shape[0] // 2
    return pl.pallas_call(
        functools.partial(modes_kernel, groups),
        out_shape=jax.ShapeDtypeStruct((orders, groups * R_DEV * 4 // 128, 128), jnp.float32),
        name="modes",
    )(rows, owners, keys, waves)


def harmonics_kernel(in_ref, out_ref):
    total = jnp.sum(in_ref[...], axis=0) * (1.0 / math.sqrt(NPHI))
    row = lax.broadcasted_iota(jnp.int32, total.shape, 0)
    total = jnp.where((row & 2) == 0, total, -total)
    out_ref[...] = jnp.broadcast_to(total[None], out_ref.shape).astype(out_ref.dtype)


def harmonics_for_all(arrived, copies):
    return pl.pallas_call(
        harmonics_kernel,
        out_shape=jax.ShapeDtypeStruct((copies, *arrived.shape[1:]), jnp.bfloat16),
        in_specs=[pl.BlockSpec(memory_space=pltpu.VMEM)],
        name="harmonics",
    )(in_vmem(arrived))


def legendre_kernel(first_ref, modes_ref, leg_ref, even_hbm, odd_hbm, out_ref, even, odd, sem):
    even_copy = pltpu.make_async_copy(even_hbm, even, sem.at[0])
    odd_copy = pltpu.make_async_copy(odd_hbm, odd, sem.at[1])
    even_copy.start()
    odd_copy.start()
    blocks, rows = modes_ref.shape[0], modes_ref.shape[1]
    pieces = []
    for block in range(blocks):
        value = modes_ref[block].astype(jnp.float32)
        for part in range(rows // 4):
            pieces.append(value[part * 4 : (part + 1) * 4])
    spectrum = jnp.concatenate(pieces, axis=1).astype(jnp.bfloat16)
    coefficients = dot32(spectrum, leg_ref[0], NT)
    width = coefficients.shape[1]
    degree = first_ref[0] + lax.broadcasted_iota(jnp.int32, (1, width), 1)
    degree = degree.astype(jnp.float32)
    smoothing = jnp.exp(-2.0 * degree * (degree + 1.0) / (L * L))
    factor = jnp.sqrt(
        jnp.maximum((degree - 1.0) * (degree + 2.0), 0.0)
        / jnp.maximum(degree * (degree + 1.0), 1.0)
    )
    trace_terms = (smoothing * coefficients).astype(jnp.bfloat16)
    shear_terms = ((-0.5 * smoothing * factor) * coefficients).astype(jnp.bfloat16)
    own = out_ref.shape[2]

    def put(kind, value):
        for block in range(blocks):
            out_ref[block, kind * 4 : kind * 4 + 4, :] = value[:, block * own : (block + 1) * own]

    put(0, dot32(trace_terms, leg_ref[0], NN))
    even_copy.wait()
    put(1, dot32(shear_terms, even[0], NN))
    odd_copy.wait()
    put(2, dot32(shear_terms, odd[0], NN))


def legendre_pair(first_degree, modes, legendre_table, spin_even, spin_odd):
    vmem = pl.BlockSpec(memory_space=pltpu.VMEM)
    left = pl.BlockSpec(memory_space=pl.ANY)
    blocks = modes.shape[0]
    cycles = legendre_table.shape[2]
    return pl.pallas_call(
        legendre_kernel,
        out_shape=jax.ShapeDtypeStruct((blocks, 12, cycles // blocks), jnp.float32),
        in_specs=[pl.BlockSpec(memory_space=pltpu.SMEM), vmem, vmem, left, left],
        out_specs=vmem,
        scratch_shapes=[
            pltpu.VMEM(spin_even.shape, spin_even.dtype),
            pltpu.VMEM(spin_odd.shape, spin_odd.dtype),
            pltpu.SemaphoreType.DMA((2,)),
        ],
        name="legendre",
    )(first_degree, in_vmem(modes), legendre_table, spin_even, spin_odd)


def fields_kernel(scale, terms_ref, order_ref, wave_ref, out_ref):
    position = pl.program_id(0)
    turn_cos, turn_sin = eighth_turn(order_ref[...] * position)
    real, imag = [], []
    for kind in range(3):
        for shell in range(2):
            cos_term, sin_term = terms_ref[kind * 4 + shell], terms_ref[kind * 4 + 2 + shell]
            real.append(-sin_term if kind == 2 else cos_term)
            imag.append(cos_term if kind == 2 else sin_term)
    real = jnp.concatenate(real, axis=0)
    imag = jnp.concatenate(imag, axis=0)
    turned = jnp.concatenate(
        [real * turn_cos - imag * turn_sin, -(real * turn_sin + imag * turn_cos)], axis=1
    )
    t_high, t_low = halves(turned)
    w_high, w_low = halves(wave_ref[...])
    fields = (dot32(t_high, w_high, NN) + (dot32(t_high, w_low, NN) + dot32(t_low, w_high, NN))) * scale
    fields = fields.reshape(3, 2, R_DEV, SEG)
    for shell in range(2):
        half_trace = 0.5 * fields[0, shell]
        first, second = fields[1, shell], fields[2, shell]
        size = jnp.sqrt(first * first + second * second)
        out_ref[0, shell, 0] = half_trace + size
        out_ref[1, shell, 0] = half_trace - size


def eigenvalues(terms, azimuth_orders, waves):
    orders = azimuth_orders.shape[0]
    whole = lambda *shape: pl.BlockSpec(shape, lambda p: (0,) * len(shape))
    return pl.pallas_call(
        functools.partial(fields_kernel, 2.0 / math.sqrt(orders)),
        out_shape=jax.ShapeDtypeStruct((2, 2, 1, R_DEV, NPHI), jnp.float32),
        grid=(POS,),
        in_specs=[whole(12, R_DEV, orders), whole(1, orders), whole(2 * orders, SEG)],
        out_specs=pl.BlockSpec((2, 2, 1, R_DEV, SEG), lambda p: (0, 0, 0, 0, p)),
        name="fields",
        compiler_params=room(16),
    )(terms, azimuth_orders[None], waves)


def shifted(x, axis, by):
    size = lax.axis_size(axis)
    return lax.ppermute(x, axis, [(i, (i + by) % size) for i in range(size)])


def add_kernel(up_ref, down_ref, up_own_ref, down_own_ref, up_out, down_out):
    size, whole = up_ref.shape[0], up_own_ref.shape[0]
    for lead, moving_ref, own_ref, out in (
        (0, up_ref, up_own_ref, up_out),
        (whole - size, down_ref, down_own_ref, down_out),
    ):
        if size < whole:
            other = size - lead
            out[other : other + size] = own_ref[other : other + size].astype(out.dtype)
        added = own_ref[lead : lead + size] + moving_ref[...].astype(jnp.float32)
        out[lead : lead + size] = added.astype(out.dtype)


def in_vmem(x):
    return pltpu.with_memory_space_constraint(x, pltpu.VMEM)


def ring_add(*operands):
    vmem = pl.BlockSpec(memory_space=pltpu.VMEM)
    result = pltpu.VMEM(operands[2].shape, operands[0].dtype)
    return pl.pallas_call(
        add_kernel,
        out_shape=(result, result),
        in_specs=[vmem] * 4,
        out_specs=(vmem, vmem),
        name="ring_add",
        compiler_params=room(8),
    )(*[in_vmem(x) if x.shape == operands[0].shape else x for x in operands])


def ring_sums(chunks, far, axis, token):
    size = len(chunks)
    middle = size // 2
    up, down = far
    for distance in range(middle - 1, -1, -1):
        up = shifted(up, axis, 1)
        down = shifted(down, axis, -1)
        if distance > 0:
            own = chunks[distance]
            if distance == middle - 1:
                own = after(own, token)
            up, down = ring_add(up, down, own, chunks[size - distance])
    return chunks[0], up, down


def after(x, token):
    return lax.optimization_barrier((x, token))[0]


DIGIT = 64
TILE = 256
EXTRA = 16


def pack_kernel(rows_ref, owner_ref, key_ref, *outs):
    size, lanes = rows_ref.shape[0] // len(outs), rows_ref.shape[1]
    key = key_ref[...]
    place = (key & 64) + (key & 7) * R_DEV + ((key >> 3) & 7)
    slot = owner_ref[...] * KEYS + place
    row = lax.broadcasted_iota(jnp.int32, (EXTRA, size), 0)
    for part, out in enumerate(outs):
        own = slot[:, part * size : (part + 1) * size]
        tail = jnp.where(row == 0, own // DIGIT, jnp.where(row == 1, own % DIGIT, 0))
        out[:size] = rows_ref[part * size : (part + 1) * size]
        out[size:] = jnp.zeros((EXTRA, lanes), out.dtype)
        out[size:, :size] = tail.astype(jnp.float32).astype(out.dtype)


def row_pieces(rows, owners, keys, parts):
    piece = jax.ShapeDtypeStruct((rows.shape[0] // parts + EXTRA, rows.shape[1]), rows.dtype)
    return pl.pallas_call(pack_kernel, out_shape=(piece,) * parts, name="pack")(
        rows, owners[None], keys[None]
    )


def sums_kernel(count, has_base, columns, rings, place_ref, *refs):
    pieces, tails = refs[:count], refs[count : 2 * count]
    outs, pick_ref = refs[2 * count + has_base : -1], refs[-1]
    slots = pick_ref.shape[0]
    size = pieces[0].shape[0]

    @pl.when(pl.program_id(0) == 0)
    def _():
        my_z, my_y = place_ref[0], place_ref[1]
        for index, tail_ref in enumerate(tails):
            tail = tail_ref[:, :size].astype(jnp.float32).astype(jnp.int32)
            slot = tail[0:1] * DIGIT + tail[1:2]
            owner = slot // KEYS
            distance = (owner // columns - my_z) & (rings - 1)
            mine = distance * KEYS + (slot & (KEYS - 1))
            mine = jnp.where((owner & (columns - 1)) == my_y, mine, -1)
            pick = lax.broadcasted_iota(jnp.int32, (slots, size), 0) == mine
            pick_ref[:, index * size : (index + 1) * size] = jnp.where(pick, 1.0, 0.0).astype(
                jnp.bfloat16
            )

    total = refs[2 * count][...] if has_base else 0.0
    for index, piece in enumerate(pieces):
        total = total + dot32(pick_ref[:, index * size : (index + 1) * size], piece[...], NN)
    start = 0
    for out in outs:
        out[...] = total[start : start + out.shape[0]].astype(out.dtype)
        start += out.shape[0]


def sum_pieces(pieces, base, place, outs):
    columns, rings = lax.axis_size(BLK[1]), lax.axis_size(BLK[0])
    size, lanes = pieces[0].shape[0] - EXTRA, pieces[0].shape[1]
    slots = rings * KEYS
    specs = [pl.BlockSpec(memory_space=pltpu.SMEM)]
    specs += [pl.BlockSpec((size, TILE), lambda n: (0, n)) for _ in pieces]
    specs += [pl.BlockSpec((EXTRA, lanes), lambda n: (size // EXTRA, 0)) for _ in pieces]
    operands = [*pieces, *pieces]
    if base is not None:
        specs.append(pl.BlockSpec((slots, TILE), lambda n: (0, n)))
        operands.append(base)
    return pl.pallas_call(
        functools.partial(sums_kernel, len(pieces), int(base is not None), columns, rings),
        out_shape=tuple(jax.ShapeDtypeStruct((rows, lanes), dtype) for rows, dtype in outs),
        grid=(lanes // TILE,),
        in_specs=specs,
        out_specs=tuple(pl.BlockSpec((rows, TILE), lambda n: (0, n)) for rows, _ in outs),
        scratch_shapes=[pltpu.VMEM((slots, size * len(pieces)), jnp.bfloat16)],
    )(place, *operands)


class ColumnSums:
    def __init__(self, rows, owners, keys, waves):
        axis = BLK[1]
        self.place = jnp.stack([lax.axis_index(BLK[0]), lax.axis_index(BLK[1])]).astype(jnp.int32)
        self.pieces = first, last = row_pieces(rows, owners, keys, 2)
        self.up = [shifted(first, axis, 1), shifted(last, axis, 1)]
        self.down = [shifted(after(last, waves), axis, -1), shifted(first, axis, -1)]

    def forward(self, token):
        self.up_far = shifted(after(self.up[0], token), BLK[1], 1)
        self.down_far = shifted(after(self.down[0], token), BLK[1], -1)

    def finish(self, token):
        rings = lax.axis_size(BLK[0])
        whole = [(rings * KEYS, jnp.float32)]
        (sums,) = sum_pieces(self.pieces, None, self.place, whole)
        near, following = [self.up[0], self.down[0]], [self.up[1], self.down[1]]
        (sums,) = sum_pieces(near, sums, self.place, whole)
        (sums,) = sum_pieces(following, sums, self.place, whole)
        one, half = (KEYS, jnp.float32), (KEYS // 2, jnp.bfloat16)
        side = [one] * (rings // 2)
        outs = [*side, half, half, *side[1:]]
        parts = sum_pieces([self.up_far, self.down_far], sums, self.place, outs)
        middle = rings // 2
        chunks = [*parts[:middle], None, *parts[middle + 2 :]]
        return ring_sums(chunks, parts[middle : middle + 2], BLK[0], token)


def maps_kernel(own, up, down, out_ref):
    for shell in range(2):
        for position in range(POS):
            row = pl.ds((shell * POS + position) * R_DEV, R_DEV)
            total = own[row] + up[row].astype(jnp.float32) + down[row].astype(jnp.float32)
            out_ref[shell, 0, :, position * SEG : (position + 1) * SEG] = total


def map_output(own, up, down):
    vmem = pl.BlockSpec(memory_space=pltpu.VMEM)
    return pl.pallas_call(
        maps_kernel,
        out_shape=jax.ShapeDtypeStruct((2, 1, R_DEV, NPHI), jnp.float32),
        in_specs=[vmem] * 3,
        name="maps",
        compiler_params=room(8),
    )(in_vmem(own), in_vmem(up), in_vmem(down))


def body(partial_rows, row_owner, row_key, azimuth_orders, legendre_table, spin_even, spin_odd):
    groups = lax.axis_size(BLK)
    blocks = lax.axis_size("lblk")
    rows = partial_rows[0]
    owners = row_owner[0, :, 0]
    keys = row_key[0]
    orders = azimuth_orders.shape[0]
    waves = wave_tables(azimuth_orders)

    columns = ColumnSums(rows, owners, keys, waves)
    sums = local_modes(rows, owners[None], keys[None], waves, groups)
    arrived = lax.all_to_all(sums, BLK, split_axis=0, concat_axis=0, tiled=True)
    columns.forward(arrived)
    modes = harmonics_for_all(arrived, blocks)
    modes = lax.all_to_all(modes, "lblk", 0, 0, tiled=True)
    first_degree = (lax.axis_index("lblk") * legendre_table.shape[1]).astype(jnp.int32)[None]
    pieces = legendre_pair(first_degree, modes, legendre_table, spin_even, spin_odd)
    pieces = lax.all_to_all(pieces, "lblk", split_axis=0, concat_axis=0, tiled=True)
    summed = pieces.sum(axis=0).astype(jnp.bfloat16)
    summed = summed.reshape(12, groups, R_DEV).transpose(1, 0, 2).reshape(groups, 12 * R_DEV)
    returned = lax.all_to_all(summed, BLK, split_axis=0, concat_axis=0, tiled=True)
    terms = returned.astype(jnp.float32).T.reshape(12, R_DEV, orders)
    eigen = eigenvalues(terms, azimuth_orders, waves)
    return (eigen, map_output(*columns.finish(returned)))


def solution(mesh):
    finer = Mesh(mesh.devices.reshape(8, 4, mesh.shape["lblk"]), ("blk_0", "blk_1", "lblk"))
    placed = (
        P("lblk", BLK, None),
        P("lblk", BLK, None),
        P("lblk", BLK),
        P(),
        P(BLK, "lblk", None),
        P(BLK, "lblk", None),
        P(BLK, "lblk", None),
    )
    return jax.shard_map(
        body,
        mesh=finer,
        in_specs=placed,
        out_specs=(P(None, None, "lblk", BLK, None), P(None, "lblk", BLK, None)),
        check_vma=False,
    )
```

```python
import functools
import math

import jax
import jax.numpy as jnp
from jax import lax
from jax.experimental import pallas as pl
from jax.experimental.pallas import tpu as pltpu
from jax.sharding import Mesh
from jax.sharding import PartitionSpec as P


NPHI = 8192
L = 4096
SEG = 1024
R_DEV = 8
PR = 1024
KEYS = 128
POS = NPHI // SEG
BLK = ("blk_0", "blk_1")

NT = (((1,), (1,)), ((), ()))
NN = (((1,), (0,)), ((), ()))


def room(mebibytes):
    return pltpu.CompilerParams(vmem_limit_bytes=mebibytes << 20)


def halves(x):
    high = x.astype(jnp.bfloat16)
    low = (x - high.astype(jnp.float32)).astype(jnp.bfloat16)
    return high, low


def dot32(a, b, dims):
    return lax.dot_general(a, b, dims, preferred_element_type=jnp.float32)


def wave_tables(azimuth_orders):
    orders = azimuth_orders.shape[0]
    trig = lax.broadcasted_iota(jnp.int32, (2, orders, SEG), 0)
    pixel = lax.broadcasted_iota(jnp.int32, (2, orders, SEG), 2)
    phase = pixel * azimuth_orders[None, :, None] - trig * (NPHI // 4)
    angles = (phase & (NPHI - 1)).astype(jnp.float32) * (2.0 * math.pi / NPHI)
    return jnp.cos(angles).reshape(2 * orders, SEG)


def eighth_turn(index):
    angle = (index & (POS - 1)).astype(jnp.float32) * (2.0 * math.pi / POS)
    return jnp.cos(angle), jnp.sin(angle)


def modes_kernel(slices, rows_ref, owner_ref, key_ref, wave_ref, out_ref):
    orders = wave_ref.shape[0] // 2
    w_high, w_low = halves(wave_ref[...])
    rows = rows_ref[...]
    seg = dot32(w_high, rows, NT) + dot32(w_low, rows, NT)
    cos_part, sin_part = seg[:orders], seg[orders:]
    key = key_ref[...]
    half = wave_ref[:, SEG // 2 : SEG // 2 + 1]
    turn_cos, turn_sin = half[:orders], half[orders:]
    for bit in range(3):
        turn_cos, turn_sin = turn_cos * turn_cos - turn_sin * turn_sin, 2.0 * turn_cos * turn_sin
        turned = (key & (1 << bit)) != 0
        step_cos = jnp.where(turned, turn_cos, 1.0)
        step_sin = jnp.where(turned, turn_sin, 0.0)
        cos_part, sin_part = (
            cos_part * step_cos - sin_part * step_sin,
            sin_part * step_cos + cos_part * step_sin,
        )
    modes = jnp.concatenate([cos_part, sin_part], axis=0)
    cycles = slices * R_DEV
    slot = (key >> 6) * cycles + owner_ref[...] * R_DEV + ((key >> 3) & (R_DEV - 1))
    pick = lax.broadcasted_iota(jnp.int32, (2 * cycles, PR), 0) == slot
    pick = jnp.where(pick, 1.0, 0.0).astype(jnp.bfloat16)
    m_high, m_low = halves(modes)
    sums = dot32(m_high, pick, NT) + dot32(m_low, pick, NT)
    parts = cycles // 128
    for trig in range(2):
        for shell in range(2):
            for part in range(parts):
                out_ref[:, part * 4 + trig * 2 + shell, :] = sums[
                    trig * orders : (trig + 1) * orders,
                    shell * cycles + part * 128 : shell * cycles + (part + 1) * 128,
                ]


def local_modes(rows, owners, keys, waves, groups):
    orders = waves.shape[0] // 2
    return pl.pallas_call(
        functools.partial(modes_kernel, groups),
        out_shape=jax.ShapeDtypeStruct((orders, groups * R_DEV * 4 // 128, 128), jnp.float32),
        name="modes",
    )(rows, owners, keys, waves)


def harmonics_kernel(in_ref, out_ref):
    total = jnp.sum(in_ref[...], axis=0) * (1.0 / math.sqrt(NPHI))
    row = lax.broadcasted_iota(jnp.int32, total.shape, 0)
    total = jnp.where((row & 2) == 0, total, -total)
    out_ref[...] = jnp.broadcast_to(total[None], out_ref.shape).astype(out_ref.dtype)


def harmonics_for_all(arrived, copies):
    return pl.pallas_call(
        harmonics_kernel,
        out_shape=jax.ShapeDtypeStruct((copies, *arrived.shape[1:]), jnp.bfloat16),
        in_specs=[pl.BlockSpec(memory_space=pltpu.VMEM)],
        name="harmonics",
    )(in_vmem(arrived))


def legendre_kernel(first_ref, modes_ref, leg_ref, even_hbm, odd_hbm, out_ref, even, odd, sem):
    even_copy = pltpu.make_async_copy(even_hbm, even, sem.at[0])
    odd_copy = pltpu.make_async_copy(odd_hbm, odd, sem.at[1])
    even_copy.start()
    odd_copy.start()
    blocks, rows = modes_ref.shape[0], modes_ref.shape[1]
    pieces = []
    for block in range(blocks):
        value = modes_ref[block].astype(jnp.float32)
        for part in range(rows // 4):
            pieces.append(value[part * 4 : (part + 1) * 4])
    spectrum = jnp.concatenate(pieces, axis=1).astype(jnp.bfloat16)
    coefficients = dot32(spectrum, leg_ref[0], NT)
    width = coefficients.shape[1]
    degree = first_ref[0] + lax.broadcasted_iota(jnp.int32, (1, width), 1)
    degree = degree.astype(jnp.float32)
    smoothing = jnp.exp(-2.0 * degree * (degree + 1.0) / (L * L))
    factor = jnp.sqrt(
        jnp.maximum((degree - 1.0) * (degree + 2.0), 0.0)
        / jnp.maximum(degree * (degree + 1.0), 1.0)
    )
    trace_terms = (smoothing * coefficients).astype(jnp.bfloat16)
    shear_terms = ((-0.5 * smoothing * factor) * coefficients).astype(jnp.bfloat16)
    own = out_ref.shape[2]

    def put(kind, value):
        for block in range(blocks):
            out_ref[block, kind * 4 : kind * 4 + 4, :] = value[:, block * own : (block + 1) * own]

    put(0, dot32(trace_terms, leg_ref[0], NN))
    even_copy.wait()
    put(1, dot32(shear_terms, even[0], NN))
    odd_copy.wait()
    put(2, dot32(shear_terms, odd[0], NN))


def legendre_pair(first_degree, modes, legendre_table, spin_even, spin_odd):
    vmem = pl.BlockSpec(memory_space=pltpu.VMEM)
    left = pl.BlockSpec(memory_space=pl.ANY)
    blocks = modes.shape[0]
    cycles = legendre_table.shape[2]
    return pl.pallas_call(
        legendre_kernel,
        out_shape=jax.ShapeDtypeStruct((blocks, 12, cycles // blocks), jnp.float32),
        in_specs=[pl.BlockSpec(memory_space=pltpu.SMEM), vmem, vmem, left, left],
        out_specs=vmem,
        scratch_shapes=[
            pltpu.VMEM(spin_even.shape, spin_even.dtype),
            pltpu.VMEM(spin_odd.shape, spin_odd.dtype),
            pltpu.SemaphoreType.DMA((2,)),
        ],
        name="legendre",
    )(first_degree, in_vmem(modes), legendre_table, spin_even, spin_odd)


def fields_kernel(scale, terms_ref, order_ref, wave_ref, out_ref):
    position = pl.program_id(0)
    turn_cos, turn_sin = eighth_turn(order_ref[...] * position)
    real, imag = [], []
    for kind in range(3):
        for shell in range(2):
            cos_term, sin_term = terms_ref[kind * 4 + shell], terms_ref[kind * 4 + 2 + shell]
            real.append(-sin_term if kind == 2 else cos_term)
            imag.append(cos_term if kind == 2 else sin_term)
    real = jnp.concatenate(real, axis=0)
    imag = jnp.concatenate(imag, axis=0)
    turned = jnp.concatenate(
        [real * turn_cos - imag * turn_sin, -(real * turn_sin + imag * turn_cos)], axis=1
    )
    t_high, t_low = halves(turned)
    w_high, w_low = halves(wave_ref[...])
    fields = (dot32(t_high, w_high, NN) + (dot32(t_high, w_low, NN) + dot32(t_low, w_high, NN))) * scale
    fields = fields.reshape(3, 2, R_DEV, SEG)
    for shell in range(2):
        half_trace = 0.5 * fields[0, shell]
        first, second = fields[1, shell], fields[2, shell]
        size = jnp.sqrt(first * first + second * second)
        out_ref[0, shell, 0] = half_trace + size
        out_ref[1, shell, 0] = half_trace - size


def eigenvalues(terms, azimuth_orders, waves):
    orders = azimuth_orders.shape[0]
    whole = lambda *shape: pl.BlockSpec(shape, lambda p: (0,) * len(shape))
    return pl.pallas_call(
        functools.partial(fields_kernel, 2.0 / math.sqrt(orders)),
        out_shape=jax.ShapeDtypeStruct((2, 2, 1, R_DEV, NPHI), jnp.float32),
        grid=(POS,),
        in_specs=[whole(12, R_DEV, orders), whole(1, orders), whole(2 * orders, SEG)],
        out_specs=pl.BlockSpec((2, 2, 1, R_DEV, SEG), lambda p: (0, 0, 0, 0, p)),
        name="fields",
        compiler_params=room(16),
    )(terms, azimuth_orders[None], waves)


def shifted(x, axis, by):
    size = lax.axis_size(axis)
    return lax.ppermute(x, axis, [(i, (i + by) % size) for i in range(size)])


def add_kernel(up_ref, down_ref, up_own_ref, down_own_ref, up_out, down_out):
    size, whole = up_ref.shape[0], up_own_ref.shape[0]
    for lead, moving_ref, own_ref, out in (
        (0, up_ref, up_own_ref, up_out),
        (whole - size, down_ref, down_own_ref, down_out),
    ):
        if size < whole:
            other = size - lead
            out[other : other + size] = own_ref[other : other + size].astype(out.dtype)
        added = own_ref[lead : lead + size] + moving_ref[...].astype(jnp.float32)
        out[lead : lead + size] = added.astype(out.dtype)


def in_vmem(x):
    return pltpu.with_memory_space_constraint(x, pltpu.VMEM)


def fetch_add_kernel(up_ref, down_ref, up_hbm, down_hbm, up_out, down_out, up_own, down_own, sems):
    copies = [
        pltpu.make_async_copy(up_hbm, up_own, sems.at[0]),
        pltpu.make_async_copy(down_hbm, down_own, sems.at[1]),
    ]
    for copy in copies:
        copy.start()
    for copy in copies:
        copy.wait()
    add_kernel(up_ref, down_ref, up_own, down_own, up_out, down_out)


def first_ring_add(up, down, up_own, down_own):
    vmem = pl.BlockSpec(memory_space=pltpu.VMEM)
    hbm = pl.BlockSpec(memory_space=pltpu.HBM)
    result = pltpu.VMEM(up_own.shape, up.dtype)
    own = pltpu.VMEM(up_own.shape, up_own.dtype)
    return pl.pallas_call(
        fetch_add_kernel,
        out_shape=(result, result),
        in_specs=[vmem, vmem, hbm, hbm],
        out_specs=(vmem, vmem),
        scratch_shapes=[own, own, pltpu.SemaphoreType.DMA((2,))],
        name="ring_add_first",
    )(in_vmem(up), in_vmem(down), up_own, down_own)


def ring_add(*operands):
    vmem = pl.BlockSpec(memory_space=pltpu.VMEM)
    result = pltpu.VMEM(operands[2].shape, operands[0].dtype)
    return pl.pallas_call(
        add_kernel,
        out_shape=(result, result),
        in_specs=[vmem] * 4,
        out_specs=(vmem, vmem),
        name="ring_add",
        compiler_params=room(8),
    )(*[in_vmem(x) if x.shape == operands[0].shape else x for x in operands])


def ring_sums(chunks, far, axis, token):
    size = len(chunks)
    middle = size // 2
    up, down = far
    for distance in range(middle - 1, -1, -1):
        up = shifted(up, axis, 1)
        down = shifted(down, axis, -1)
        if distance > 0:
            own = chunks[distance]
            if distance == middle - 1:
                own = after(own, token)
            add = first_ring_add if distance == middle - 1 else ring_add
            up, down = add(up, down, own, chunks[size - distance])
    return chunks[0], up, down


def after(x, token):
    return lax.optimization_barrier((x, token))[0]


DIGIT = 64
TILE = 256
EXTRA = 16


def pack_kernel(rows_ref, owner_ref, key_ref, *outs):
    size, lanes = rows_ref.shape[0] // len(outs), rows_ref.shape[1]
    key = key_ref[...]
    place = (key & 64) + (key & 7) * R_DEV + ((key >> 3) & 7)
    slot = owner_ref[...] * KEYS + place
    row = lax.broadcasted_iota(jnp.int32, (EXTRA, size), 0)
    for part, out in enumerate(outs):
        own = slot[:, part * size : (part + 1) * size]
        tail = jnp.where(row == 0, own // DIGIT, jnp.where(row == 1, own % DIGIT, 0))
        out[:size] = rows_ref[part * size : (part + 1) * size]
        out[size:] = jnp.zeros((EXTRA, lanes), out.dtype)
        out[size:, :size] = tail.astype(jnp.float32).astype(out.dtype)


def row_pieces(rows, owners, keys, parts):
    piece = jax.ShapeDtypeStruct((rows.shape[0] // parts + EXTRA, rows.shape[1]), rows.dtype)
    return pl.pallas_call(pack_kernel, out_shape=(piece,) * parts, name="pack")(
        rows, owners[None], keys[None]
    )


def sums_kernel(count, has_base, columns, rings, place_ref, *refs):
    pieces, tails = refs[:count], refs[count : 2 * count]
    outs, pick_ref = refs[2 * count + has_base : -1], refs[-1]
    slots = pick_ref.shape[0]
    size = pieces[0].shape[0]

    @pl.when(pl.program_id(0) == 0)
    def _():
        my_z, my_y = place_ref[0], place_ref[1]
        for index, tail_ref in enumerate(tails):
            tail = tail_ref[:, :size].astype(jnp.float32).astype(jnp.int32)
            slot = tail[0:1] * DIGIT + tail[1:2]
            owner = slot // KEYS
            distance = (owner // columns - my_z) & (rings - 1)
            mine = distance * KEYS + (slot & (KEYS - 1))
            mine = jnp.where((owner & (columns - 1)) == my_y, mine, -1)
            pick = lax.broadcasted_iota(jnp.int32, (slots, size), 0) == mine
            pick_ref[:, index * size : (index + 1) * size] = jnp.where(pick, 1.0, 0.0).astype(
                jnp.bfloat16
            )

    total = refs[2 * count][...] if has_base else 0.0
    for index, piece in enumerate(pieces):
        total = total + dot32(pick_ref[:, index * size : (index + 1) * size], piece[...], NN)
    start = 0
    for out in outs:
        out[...] = total[start : start + out.shape[0]].astype(out.dtype)
        start += out.shape[0]


def sum_pieces(pieces, base, place, outs):
    columns, rings = lax.axis_size(BLK[1]), lax.axis_size(BLK[0])
    size, lanes = pieces[0].shape[0] - EXTRA, pieces[0].shape[1]
    slots = rings * KEYS
    specs = [pl.BlockSpec(memory_space=pltpu.SMEM)]
    specs += [pl.BlockSpec((size, TILE), lambda n: (0, n)) for _ in pieces]
    specs += [pl.BlockSpec((EXTRA, lanes), lambda n: (size // EXTRA, 0)) for _ in pieces]
    operands = [*pieces, *pieces]
    if base is not None:
        specs.append(pl.BlockSpec((slots, TILE), lambda n: (0, n)))
        operands.append(base)
    return pl.pallas_call(
        functools.partial(sums_kernel, len(pieces), int(base is not None), columns, rings),
        out_shape=tuple(jax.ShapeDtypeStruct((rows, lanes), dtype) for rows, dtype in outs),
        grid=(lanes // TILE,),
        in_specs=specs,
        out_specs=tuple(pl.BlockSpec((rows, TILE), lambda n: (0, n)) for rows, _ in outs),
        scratch_shapes=[pltpu.VMEM((slots, size * len(pieces)), jnp.bfloat16)],
    )(place, *operands)


class ColumnSums:
    def __init__(self, rows, owners, keys, waves):
        axis = BLK[1]
        self.place = jnp.stack([lax.axis_index(BLK[0]), lax.axis_index(BLK[1])]).astype(jnp.int32)
        self.pieces = first, last = row_pieces(rows, owners, keys, 2)
        self.up = [shifted(first, axis, 1), shifted(last, axis, 1)]
        self.down = [shifted(after(last, waves), axis, -1), shifted(first, axis, -1)]

    def forward(self, token):
        self.up_far = shifted(after(self.up[0], token), BLK[1], 1)
        self.down_far = shifted(after(self.down[0], token), BLK[1], -1)

    def finish(self, token):
        rings = lax.axis_size(BLK[0])
        whole = [(rings * KEYS, jnp.float32)]
        (sums,) = sum_pieces(self.pieces, None, self.place, whole)
        near, following = [self.up[0], self.down[0]], [self.up[1], self.down[1]]
        (sums,) = sum_pieces(near, sums, self.place, whole)
        (sums,) = sum_pieces(following, sums, self.place, whole)
        one, half = (KEYS, jnp.float32), (KEYS // 2, jnp.bfloat16)
        side = [one] * (rings // 2)
        outs = [*side, half, half, *side[1:]]
        parts = sum_pieces([self.up_far, self.down_far], sums, self.place, outs)
        middle = rings // 2
        chunks = [*parts[:middle], None, *parts[middle + 2 :]]
        return ring_sums(chunks, parts[middle : middle + 2], BLK[0], token)


def maps_kernel(own, up, down, out_ref):
    for shell in range(2):
        for position in range(POS):
            row = pl.ds((shell * POS + position) * R_DEV, R_DEV)
            total = own[row] + up[row].astype(jnp.float32) + down[row].astype(jnp.float32)
            out_ref[shell, 0, :, position * SEG : (position + 1) * SEG] = total


def map_output(own, up, down):
    vmem = pl.BlockSpec(memory_space=pltpu.VMEM)
    return pl.pallas_call(
        maps_kernel,
        out_shape=jax.ShapeDtypeStruct((2, 1, R_DEV, NPHI), jnp.float32),
        in_specs=[vmem] * 3,
        name="maps",
        compiler_params=room(8),
    )(in_vmem(own), in_vmem(up), in_vmem(down))


def body(partial_rows, row_owner, row_key, azimuth_orders, legendre_table, spin_even, spin_odd):
    groups = lax.axis_size(BLK)
    blocks = lax.axis_size("lblk")
    rows = partial_rows[0]
    owners = row_owner[0, :, 0]
    keys = row_key[0]
    orders = azimuth_orders.shape[0]
    waves = wave_tables(azimuth_orders)

    columns = ColumnSums(rows, owners, keys, waves)
    sums = local_modes(rows, owners[None], keys[None], waves, groups)
    arrived = lax.all_to_all(sums, BLK, split_axis=0, concat_axis=0, tiled=True)
    columns.forward(arrived)
    modes = harmonics_for_all(arrived, blocks)
    modes = lax.all_to_all(modes, "lblk", 0, 0, tiled=True)
    first_degree = (lax.axis_index("lblk") * legendre_table.shape[1]).astype(jnp.int32)[None]
    pieces = legendre_pair(first_degree, modes, legendre_table, spin_even, spin_odd)
    pieces = lax.all_to_all(pieces, "lblk", split_axis=0, concat_axis=0, tiled=True)
    summed = pieces.sum(axis=0).astype(jnp.bfloat16)
    summed = summed.reshape(12, groups, R_DEV).transpose(1, 0, 2).reshape(groups, 12 * R_DEV)
    returned = lax.all_to_all(summed, BLK, split_axis=0, concat_axis=0, tiled=True)
    terms = returned.astype(jnp.float32).T.reshape(12, R_DEV, orders)
    eigen = eigenvalues(terms, azimuth_orders, waves)
    return (eigen, map_output(*columns.finish(returned)))


def solution(mesh):
    finer = Mesh(mesh.devices.reshape(8, 4, mesh.shape["lblk"]), ("blk_0", "blk_1", "lblk"))
    placed = (
        P("lblk", BLK, None),
        P("lblk", BLK, None),
        P("lblk", BLK),
        P(),
        P(BLK, "lblk", None),
        P(BLK, "lblk", None),
        P(BLK, "lblk", None),
    )
    return jax.shard_map(
        body,
        mesh=finer,
        in_specs=placed,
        out_specs=(P(None, None, "lblk", BLK, None), P(None, "lblk", BLK, None)),
        check_vma=False,
    )
```
